32 devices in a mesh: dp: 16 (over z, x, core), tensor: 2 (over y).
Axes of the slice: x: 2, y: 2, z: 4, core: 2. Of those that a mesh axis runs over, the one named last changes fastest.
Arguments:
- inputs: bfloat16 [2, 4096, 1024], P(None, 'dp'), may hold values from -6 to 6
- cotangent: bfloat16 [2, 4096, 1024], P(None, 'dp'), may hold values from -6 to 6
- lengths: int32 [2, 16, 4], P(None, 'dp'), may hold values from 1 to 192, 256 in all within a row
- dealing: int32 [2, 256], replicated, may hold values from 0 to 255, as said below
- w_qkv: bfloat16 [3, 1024, 1024], P(None, None, 'tensor'), may hold values from -0.1875 to 0.1875
- w_out: bfloat16 [1024, 1024], P('tensor'), may hold values from -0.75 to 0.75
- w_gate_up: bfloat16 [2, 1024, 2816], P(None, None, 'tensor'), may hold values from -0.1875 to 0.1875
- w_down: bfloat16 [2816, 1024], P('tensor'), may hold values from -0.109375 to 0.109375
- gain_attn: float32 [1024], replicated, may hold values from 0.1 to 1.9
- gain_ffn: float32 [1024], replicated, may hold values from 0.1 to 1.9
Outputs:
- output: bfloat16 [2, 4096, 1024], P(None, 'dp')
- input_grad: bfloat16 [2, 4096, 1024], P(None, 'dp')
- grad_qkv: float32 [3, 1024, 1024], P(None, 'dp', 'tensor')
- grad_out: float32 [1024, 1024], P('tensor', 'dp')
- grad_gate_up: float32 [2, 1024, 2816], P(None, 'dp', 'tensor')
- grad_down: float32 [2816, 1024], P('tensor', 'dp')
- grad_gain_attn: float32 [1024], P('dp')
- grad_gain_ffn: float32 [1024], P('dp')
The draws below stay inside these ranges and needn't reach their ends.
Inputs may be any that keep to these rules, and one draw needn't show every extreme that they name: Arrival piece a holds arrival rows a * 16 to a * 16 + 15 of its micro-batch; dealing[m] is a permutation of the 256 destination pieces, and destination piece p is slot p % 16 of group p // 16, so each group receives exactly 16 pieces. The 16 arrival pieces held by one dp index send at most 2 pieces to any one group, and exactly 2 to some groups. The lengths of one group's sequences in one micro-batch sum to 256; the longest of them has exactly 192.
All inputs are finite; a program needn't handle non-finite values.
Results may differ from the reference program's by a relative error of at most 0.015.
Values may be sent and summed in bfloat16 or wider, within the bound.
No kernel may reach another device: no remote copies, remote signals or barrier semaphores. Data moves between devices by JAX's collectives and lax.ppermute only.
A program may use at most 192 MiB of HBM per device.

```python
import math
import jax
import jax.numpy as jnp
import numpy as np
from jax import lax

D = 1024
HEADS = 16
HEAD_DIM = 64
FF = 2816
GROUP = 256
MICRO = 2
SEQS = 4
MOST_LEN = 192
GROUPS = 16
PIECE = 16
TOKENS = 4096


def permute_one(sub_key):
    return jax.random.permutation(sub_key, GROUPS)


def deal_micro(key):
    count = GROUPS
    keys_all = jax.random.split(key, 4)
    pairing = jax.random.permutation(keys_all[0], count).astype(jnp.int32)
    shuffles = jax.vmap(permute_one)(jax.random.split(keys_all[1], count // 2))
    placing = jnp.argsort(shuffles, axis=1).astype(jnp.int32)
    quarter = max(count // 4, 1)
    swing = jnp.where(placing < quarter, 1, jnp.where(placing < 2 * quarter, -1, 0)).astype(jnp.int32)
    pair_counts = jnp.stack([1 + swing, 1 - swing], axis=1).reshape(count, count)
    counts = jnp.zeros((count, count), jnp.int32).at[pairing].set(pair_counts)
    candidates = jnp.concatenate([jnp.arange(count), jnp.arange(count)]).astype(jnp.int32)
    copies = jnp.concatenate([jnp.zeros((count,), jnp.int32), jnp.ones((count,), jnp.int32)])

    def pick_targets(row_counts, sub_key):
        included = jnp.take(row_counts, candidates) > copies
        ranking = jnp.where(included, jax.random.permutation(sub_key, 2 * count).astype(jnp.int32), 2 * count + jnp.arange(2 * count, dtype=jnp.int32))
        return candidates[jnp.argsort(ranking)[:count]]
    targets = jax.vmap(pick_targets)(counts, jax.random.split(keys_all[2], count)).reshape(count * count)
    tie_keys = jax.random.permutation(keys_all[3], count * count).astype(jnp.int32)
    ordering = jnp.argsort(targets * (count * count) + tie_keys)
    slots = jnp.zeros((count * count,), jnp.int32).at[ordering].set(jnp.arange(count * count, dtype=jnp.int32) - targets[ordering] * count)
    return (targets * count + slots).astype(jnp.int32)


def draw_dealing(key, part):
    return jax.vmap(deal_micro)(jax.random.split(key, MICRO))


def block_scale(own_key, dims, pieces, smallest, high):
    def one(dim, parts):
        steps = jax.random.uniform(jax.random.fold_in(jax.random.fold_in(own_key, 6), dim), (parts,), jnp.float32, smallest / len(pieces), high / len(pieces))
        return jnp.repeat(jnp.exp(steps), dims[dim] // parts).reshape((-1,) + (1,) * (len(dims) - dim - 1))

    level = one(*pieces[0])
    for cut in pieces[1:]:
        level = level * one(*cut)
    return level


def profile(amount, total, limit, lean):
    portions = [(1 << 20) // math.isqrt(standing ** lean) + 1 for standing in range(2, amount + 1)]
    rest, given = total - limit - (amount - 1), [1] * (amount - 1)
    while rest > 0:
        free = [i for i in range(amount - 1) if given[i] < limit]
        mass, left = sum([portions[i] for i in free]), rest
        for i in free:
            addition = min(limit - given[i], max(1, left * portions[i] // mass), rest)
            given[i] = given[i] + addition
            rest = rest - addition
    return np.array([limit] + given)


def uneven_parts(own_key, count, total, bound, lean):
    if count == 2:
        one = jax.random.randint(own_key, (), max(1, total - bound), min(bound, total - 1) + 1)
        return jnp.stack([one, total - one])
    sizes = jnp.asarray(profile(count, total, bound, lean), jnp.int32)
    pairs = (count - 1) // 2
    giver, sink = sizes[1:1 + 2 * pairs:2], sizes[2:2 + 2 * pairs:2]
    room = jnp.minimum(giver - 1, bound - sink)
    passed = jax.random.randint(jax.random.fold_in(own_key, 1), (pairs,), 0, 1 << 20) % (room + 1)
    sizes = sizes.at[1:1 + 2 * pairs:2].set(giver - passed).at[2:2 + 2 * pairs:2].set(sink + passed)
    return sizes[jax.random.permutation(jax.random.fold_in(own_key, 2), count)]


def centred(key, shape, deviation, most, cuts=(), held_as=jnp.bfloat16):
    loudness = block_scale(key, shape, cuts, -0.22, 0.18) if cuts else 1.0
    array = jax.random.normal(key, shape, jnp.float32) * deviation * loudness
    return jnp.minimum(jnp.maximum(array, -most), most).astype(held_as)


def setup_inputs(seed: int = 0) -> dict:
    streams_of = jax.random.split(jax.random.key(seed), 11)
    inputs = centred(streams_of[0], (MICRO, TOKENS, D), 1.0, 6.0, ((1, 16),))
    cotangent = centred(streams_of[1], (MICRO, TOKENS, D), 1.0, 6.0, ((1, 16),))
    lengths = jax.vmap(lambda own: uneven_parts(own, SEQS, GROUP, MOST_LEN, 2))(jax.random.split(streams_of[2], MICRO * GROUPS)).reshape((MICRO, GROUPS, SEQS)).astype(jnp.int32)
    dealing = draw_dealing(jax.random.fold_in(streams_of[10], 71), 0)
    w_qkv = centred(streams_of[4], (3, D, D), D ** -0.5, 0.1875, ((2, 2),))
    w_out = centred(streams_of[5], (D, D), (D // 16) ** -0.5, 0.75, ((0, 2),))
    w_gate_up = centred(streams_of[6], (2, D, FF), D ** -0.5, 0.1875, ((2, 2),))
    w_down = centred(streams_of[7], (FF, D), FF ** -0.5, 0.109375, ((0, 2),))
    gain_attn = jnp.clip(1.0 + 0.18 * jax.random.normal(streams_of[8], (D,), jnp.float32), 0.1, 1.9)
    gain_ffn = jnp.clip(1.0 + 0.18 * jax.random.normal(streams_of[9], (D,), jnp.float32), 0.1, 1.9)
    return {"inputs": inputs, "cotangent": cotangent, "lengths": lengths, "dealing": dealing, "w_qkv": w_qkv, "w_out": w_out, "w_gate_up": w_gate_up, "w_down": w_down, "gain_attn": gain_attn, "gain_ffn": gain_ffn}


@jax.custom_vjp
def low(v):
    return lax.optimization_barrier(v.astype(jnp.bfloat16)).astype(jnp.float32)

@jax.custom_vjp
def low_back(v):
    return v

def low_keep(v):
    return (low(v), None)

def low_pass(kept, grad):
    return (grad,)

def back_keep(v):
    return (v, None)

def back_low(kept, grad):
    return (low(grad),)
low.defvjp(low_keep, low_pass)
low_back.defvjp(back_keep, back_low)

def rms_norm(values, gain_vec):
    return values * lax.rsqrt(lax.optimization_barrier(jnp.mean(values * values, axis=-1, keepdims=True)) + 1e-05) * gain_vec

def group_layer(weights, hidden_in, seq_lengths):
    w_qkv, w_out, w_gate_up, w_down, gain_attn, gain_ffn = weights
    row_count = hidden_in.shape[0]
    places = jnp.arange(row_count, dtype=jnp.int32)
    seq_ends = jnp.cumsum(seq_lengths).astype(jnp.int32)
    segment = lax.optimization_barrier(jnp.sum((places[:, None] >= seq_ends[None, :]).astype(jnp.int32), axis=1))
    allowed = (segment[:, None] == segment[None, :]) & (places[None, :] <= places[:, None])
    normed = low(rms_norm(hidden_in, gain_attn))
    projected = low(low_back(jnp.einsum('gd,cdj->cgj', normed, w_qkv, precision=lax.Precision.HIGHEST)))
    queries = projected[0].reshape(row_count, HEADS, HEAD_DIM)
    key_rows = projected[1].reshape(row_count, HEADS, HEAD_DIM)
    value_rows = projected[2].reshape(row_count, HEADS, HEAD_DIM)
    scores = low_back(jnp.einsum('qhd,khd->hqk', queries, key_rows, precision=lax.Precision.HIGHEST) * HEAD_DIM ** (-0.5))
    scores = jnp.where(allowed[None], scores, -1e+30)
    soft_rows = low(jax.nn.softmax(scores, axis=-1))
    mixed = jnp.einsum('hqk,khd->qhd', soft_rows, value_rows, precision=lax.Precision.HIGHEST).reshape(row_count, D)
    mixed = low(low_back(mixed))
    attn_out = low_back(jnp.dot(mixed, w_out, precision=lax.Precision.HIGHEST))
    middle = hidden_in + attn_out
    normed_ffn = low(rms_norm(middle, gain_ffn))
    gate_up = low_back(jnp.einsum('gd,cdf->cgf', normed_ffn, w_gate_up, precision=lax.Precision.HIGHEST))
    activated = low(jax.nn.silu(gate_up[0]) * gate_up[1])
    return middle + low_back(jnp.dot(activated, w_down, precision=lax.Precision.HIGHEST))

def forward(inputs_f, w_qkv, w_out, w_gate_up, w_down, gain_attn, gain_ffn, gather_rows, return_rows, lengths):
    weights = (w_qkv, w_out, w_gate_up, w_down, gain_attn, gain_ffn)
    flat_in = inputs_f.reshape(MICRO * TOKENS, D)
    packed = jnp.take(flat_in, gather_rows, axis=0).reshape(MICRO * GROUPS, GROUP, D)

    def one_group(state_in, group_item):
        return (state_in, group_layer(weights, group_item[0], group_item[1]))
    unused, packed_out = lax.scan(jax.checkpoint(one_group), jnp.zeros((), jnp.float32), (packed, lengths.reshape(MICRO * GROUPS, SEQS)))
    return jnp.take(packed_out.reshape(MICRO * TOKENS, D), return_rows, axis=0).reshape(MICRO, TOKENS, D)

def reference(inputs, cotangent, lengths, dealing, w_qkv, w_out, w_gate_up, w_down, gain_attn, gain_ffn):
    arrival = jnp.arange(TOKENS, dtype=jnp.int32)
    offsets = (jnp.arange(MICRO, dtype=jnp.int32) * TOKENS)[:, None]
    return_rows = offsets + jnp.take(dealing, arrival // PIECE, axis=1) * PIECE + arrival % PIECE
    return_rows = return_rows.reshape(MICRO * TOKENS).astype(jnp.int32)
    gather_rows = jnp.zeros((MICRO * TOKENS,), jnp.int32).at[return_rows].set(jnp.arange(MICRO * TOKENS, dtype=jnp.int32))

    def wrapped(inputs_f, wq_f, wo_f, wg_f, wd_f, ga_f, gf_f):
        return forward(inputs_f, wq_f, wo_f, wg_f, wd_f, ga_f, gf_f, gather_rows, return_rows, lengths)
    result, pullback = jax.vjp(wrapped, inputs.astype(jnp.float32), w_qkv.astype(jnp.float32), w_out.astype(jnp.float32), w_gate_up.astype(jnp.float32), w_down.astype(jnp.float32), gain_attn.astype(jnp.float32), gain_ffn.astype(jnp.float32))
    grads = pullback(cotangent.astype(jnp.float32))
    return (result.astype(jnp.bfloat16), grads[0].astype(jnp.bfloat16), grads[1], grads[2], grads[3], grads[4], grads[5], grads[6])
```

```python
import jax
import jax.numpy as jnp
from jax import lax
from jax.sharding import PartitionSpec as P

HEAD_DIM = 64
F32 = jnp.float32
BF16 = jnp.bfloat16


def routes(dealing, groups, me):
    micros, total = dealing.shape
    blocks = dealing // groups
    spots = jnp.arange(groups)
    mine = lax.dynamic_slice_in_dim(blocks, me * groups, groups, axis=1)
    earlier = (mine[:, None, :] == mine[:, :, None]) & (spots[None, None, :] < spots[None, :, None])
    mine_slots = mine * 2 + jnp.sum(earlier.astype(jnp.int32), axis=2)
    arrivals = jnp.arange(total)
    hits = dealing[:, None, :] == (me * groups + spots)[None, :, None]
    source = jnp.sum(jnp.where(hits, arrivals[None, None, :], 0), axis=2)
    ahead = (
        (blocks[:, None, :] == me)
        & (arrivals[None, None, :] // groups == source[:, :, None] // groups)
        & (arrivals[None, None, :] < source[:, :, None])
    )
    recv_slots = source // groups * 2 + jnp.sum(ahead.astype(jnp.int32), axis=2)
    return mine_slots, recv_slots


def chosen_of(slots, groups):
    matches = slots[:, None, :] == jnp.arange(2 * groups)[None, :, None]
    return jnp.sum(jnp.where(matches, jnp.arange(groups)[None, None, :], 0), axis=2)


def rows_at(array, index):
    return array.at[index].get(mode="promise_in_bounds")


def deal(pieces, chosen, take_slots):
    micros, count, rows, cols = pieces.shape
    index = (chosen + jnp.arange(micros)[:, None] * count).reshape(micros, count, 2)
    index = index.transpose(1, 0, 2).reshape(-1)
    send = rows_at(pieces.reshape(micros * count, rows, cols), index)
    send = send.reshape(count, micros * 2, rows, cols)
    got = lax.all_to_all(send, "dp", 0, 0, tiled=True).reshape(count * micros * 2, rows, cols)
    place = take_slots // 2 * (2 * micros) + take_slots % 2 + jnp.arange(micros)[:, None] * 2
    return rows_at(got, place.reshape(-1)).reshape(micros, count * rows, cols)


def swap(array):
    return lax.ppermute(array, "tensor", [(0, 1), (1, 0)])


def joined(own, other, side, axis):
    first = jnp.where(side == 0, own, other)
    second = jnp.where(side == 0, other, own)
    return jnp.concatenate([first, second], axis=axis)


def norm_rows(values, gain_vec):
    inv_rms = lax.rsqrt(jnp.mean(values * values, axis=-1, keepdims=True) + 1e-05)
    return (values * inv_rms * gain_vec, inv_rms)


def norm_back(values, inv_rms, gain_vec, d_normed):
    scaled = gain_vec * d_normed
    d_values = inv_rms * scaled - values * inv_rms**3 * jnp.mean(
        scaled * values, axis=-1, keepdims=True
    )
    return (d_values, jnp.sum(d_normed * values * inv_rms, axis=0))


def bit_order(count):
    bits = count.bit_length() - 1
    order = []
    for place in range(count):
        order.append(sum(((place >> (bits - 1 - b)) & 1) << b for b in range(bits)))
    return order


def scatter_rows(whole, groups, me):
    rows, cols = whole.shape
    part = rows // groups
    bits = groups.bit_length() - 1
    split = whole.reshape((2,) * bits + (part, cols))
    current = split.transpose(tuple(range(bits - 1, -1, -1)) + (bits, bits + 1)).reshape(rows, cols)
    current = current.astype(BF16)
    for b in range(bits):
        half = current.shape[0] // 2
        bit = (me >> b) & 1
        send = lax.dynamic_slice_in_dim(current, (1 - bit) * half, half, 0)
        keep = lax.dynamic_slice_in_dim(current, bit * half, half, 0)
        got = lax.ppermute(send, "dp", [(j, j ^ (1 << b)) for j in range(groups)])
        total = keep.astype(F32) + got.astype(F32)
        current = total if b == bits - 1 else total.astype(BF16)
    return current


def high_low(vector):
    high = vector.astype(BF16)
    low = (vector - high.astype(F32)).astype(BF16)
    return high, low


def local(
    inputs, cotangent, lengths, dealing, w_qkv, w_out, w_gate_up, w_down, gain_attn, gain_ffn
):
    groups = lax.axis_size("dp")
    me = lax.axis_index("dp")
    side = lax.axis_index("tensor")
    micros, group_rows, features = inputs.shape
    piece_rows = group_rows // groups
    half_cols = features // 2
    local_cols = w_out.shape[0]
    local_heads = local_cols // HEAD_DIM
    hidden = w_down.shape[0]
    score_scale = HEAD_DIM ** (-0.5)
    places = jnp.arange(group_rows)

    mine_slots, recv_slots = routes(dealing, groups, me)
    chosen_out = chosen_of(mine_slots, groups)
    chosen_back = chosen_of(recv_slots, groups)

    def half_of(array):
        return lax.dynamic_slice_in_dim(array, side * half_cols, half_cols, axis=-1)

    def bring(array):
        pieces = half_of(array).reshape(micros, groups, piece_rows, half_cols)
        return deal(pieces, chosen_out, recv_slots)

    def give_back(array):
        pieces = array.reshape(array.shape[0], groups, piece_rows, half_cols)
        return pieces

    in_half = bring(inputs)
    co_half = bring(cotangent)
    w_out_all = joined(w_out, swap(w_out), side, 0)

    kept = []
    for m in range(micros):
        hidden_in = joined(in_half[m], swap(in_half[m]), side, 1).astype(F32)
        seq_ends = jnp.cumsum(lengths[m, 0])
        segment = jnp.sum((places[:, None] >= seq_ends[None, :]).astype(jnp.int32), axis=1)
        allowed = (segment[:, None] == segment[None, :]) & (places[None, :] <= places[:, None])
        normed_f, inv_attn = norm_rows(hidden_in, gain_attn)
        normed = normed_f.astype(BF16)
        projected = jnp.einsum(
            "gd,cdj->cgj", normed, w_qkv, preferred_element_type=F32
        ).astype(BF16)
        queries = projected[0].reshape(group_rows, local_heads, HEAD_DIM)
        key_rows = projected[1].reshape(group_rows, local_heads, HEAD_DIM)
        value_rows = projected[2].reshape(group_rows, local_heads, HEAD_DIM)
        raw = jnp.einsum("qhd,khd->hqk", queries, key_rows, preferred_element_type=F32)
        scores = jnp.where(allowed[None], raw * score_scale, -1e30)
        row_max = jnp.max(scores, axis=-1, keepdims=True)
        log_total = row_max + jnp.log(jnp.sum(jnp.exp(scores - row_max), axis=-1, keepdims=True))
        soft_f = jnp.exp(scores - log_total)
        soft_rows = soft_f.astype(BF16)
        mixed = (
            jnp.einsum("hqk,khd->qhd", soft_rows, value_rows, preferred_element_type=F32)
            .reshape(group_rows, local_cols)
            .astype(BF16)
        )
        mixed_all = joined(mixed, swap(mixed), side, 1)
        middle = hidden_in + jnp.dot(mixed_all, w_out_all, preferred_element_type=F32)
        kept.append(
            (hidden_in, normed, inv_attn, queries, key_rows, value_rows, allowed, log_total, mixed, middle)
        )

    ffn = []
    for m in range(micros):
        middle = kept[m][-1]
        upstream = joined(co_half[m], swap(co_half[m]), side, 1)
        normed2_f, inv_ffn = norm_rows(middle, gain_ffn)
        normed_ffn = normed2_f.astype(BF16)
        gate_up = jnp.einsum("gd,cdf->cgf", normed_ffn, w_gate_up, preferred_element_type=F32)
        gate_vals, up_vals = gate_up[0], gate_up[1]
        sigm = jax.nn.sigmoid(gate_vals)
        activated = (gate_vals * sigm * up_vals).astype(BF16)
        d_activated = jnp.einsum("gd,fd->gf", upstream, w_down, preferred_element_type=F32)
        d_gate = (d_activated * up_vals * sigm * (1.0 + gate_vals * (1.0 - sigm))).astype(BF16)
        d_up = (d_activated * gate_vals * sigm).astype(BF16)
        d_normed_part = jnp.dot(d_gate, w_gate_up[0].T, preferred_element_type=F32) + jnp.dot(
            d_up, w_gate_up[1].T, preferred_element_type=F32
        )
        d_normed_part = d_normed_part.astype(BF16)
        down_part = jnp.dot(activated, w_down, preferred_element_type=F32).astype(BF16)
        ffn.append((upstream, inv_ffn, normed_ffn, activated, d_gate, d_up, d_normed_part, down_part))

    out_rows = []
    for m in range(micros):
        middle, down_part = kept[m][-1], ffn[m][-1]
        theirs = lax.dynamic_slice_in_dim(down_part, (1 - side) * half_cols, half_cols, 1)
        got = swap(theirs)
        packed = half_of(middle) + (half_of(down_part).astype(F32) + got.astype(F32))
        out_rows.append(packed.astype(BF16))
    out_home = deal(
        jnp.stack(out_rows).reshape(micros, groups, piece_rows, half_cols), chosen_back, mine_slots
    )

    cat = lambda items: jnp.concatenate(items, axis=0)
    tdot = lambda a, b: lax.dot_general(a, b, (((0,), (0,)), ((), ())), preferred_element_type=F32)
    g_down = scatter_rows(tdot(cat([f[0] for f in ffn]), cat([f[3] for f in ffn])), groups, me)
    norm_all = cat([f[2] for f in ffn])
    g_gate = scatter_rows(tdot(norm_all, cat([f[4] for f in ffn])), groups, me)
    g_up = scatter_rows(tdot(norm_all, cat([f[5] for f in ffn])), groups, me)

    tail = []
    gain_a = jnp.zeros((features,), F32)
    gain_f = jnp.zeros((features,), F32)
    grad_rows = []
    for m in range(micros):
        hidden_in, normed, inv_attn, queries, key_rows, value_rows, allowed, log_total, mixed, middle = kept[m]
        upstream, inv_ffn, d_part = ffn[m][0], ffn[m][1], ffn[m][6]
        d_normed_ffn = d_part.astype(F32) + swap(d_part).astype(F32)
        d_middle_norm, g_f = norm_back(middle, inv_ffn, gain_ffn, d_normed_ffn)
        gain_f = gain_f + g_f
        d_middle = upstream.astype(F32) + d_middle_norm
        d_attn = d_middle.astype(BF16)
        d_mixed = (
            jnp.einsum("gd,jd->gj", d_attn, w_out, preferred_element_type=F32)
            .astype(BF16)
            .reshape(group_rows, local_heads, HEAD_DIM)
        )
        raw = jnp.einsum("qhd,khd->hqk", queries, key_rows, preferred_element_type=F32)
        soft_f = jnp.exp(jnp.where(allowed[None], raw * score_scale, -1e30) - log_total)
        d_probs = jnp.einsum("qhd,khd->hqk", d_mixed, value_rows, preferred_element_type=F32)
        row_dots = jnp.sum(soft_f * d_probs, axis=-1, keepdims=True)
        d_scores = (soft_f * (d_probs - row_dots)).astype(BF16)
        d_queries = (
            jnp.einsum("hqk,khd->qhd", d_scores, key_rows, preferred_element_type=F32) * score_scale
        )
        d_keys = (
            jnp.einsum("hqk,qhd->khd", d_scores, queries, preferred_element_type=F32) * score_scale
        )
        d_values = jnp.einsum(
            "hqk,qhd->khd", soft_f.astype(BF16), d_mixed, preferred_element_type=F32
        )
        d_qkv = (
            jnp.stack([d_queries, d_keys, d_values], axis=0)
            .reshape(3, group_rows, local_cols)
            .astype(BF16)
        )
        part = jnp.einsum("cgj,cdj->gd", d_qkv, w_qkv, preferred_element_type=F32).astype(BF16)
        d_normed_attn = part.astype(F32) + swap(part).astype(F32)
        d_hidden_norm, g_a = norm_back(hidden_in, inv_attn, gain_attn, d_normed_attn)
        gain_a = gain_a + g_a
        d_hidden = half_of(d_middle + d_hidden_norm).astype(BF16)
        home = deal(
            d_hidden.reshape(1, groups, piece_rows, half_cols),
            chosen_back[m : m + 1],
            mine_slots[m : m + 1],
        )
        grad_rows.append(joined(home[0], swap(home[0]), side, 1))
        tail.append((normed, d_qkv, mixed, d_attn))

    columns = list(high_low(gain_a)) + list(high_low(gain_f))
    extra = jnp.pad(jnp.stack(columns, axis=1), ((0, 0), (0, 124)))
    g_qkv = tdot(
        cat([item[0] for item in tail]),
        jnp.concatenate([cat([item[1][c] for item in tail]) for c in range(3)], axis=1),
    )
    g_out = tdot(cat([item[3] for item in tail]), cat([item[2] for item in tail]))
    g_attn = jnp.concatenate([g_qkv.astype(BF16), g_out.astype(BF16), extra], axis=1)
    g_attn = scatter_rows(g_attn, groups, me)

    out_full = jnp.stack(
        [joined(out_home[m], swap(out_home[m]), side, 1) for m in range(micros)]
    )
    grad_qkv = jnp.stack([g_attn[:, c * local_cols : (c + 1) * local_cols] for c in range(3)])
    grad_out = g_attn[:, 3 * local_cols : 4 * local_cols].T
    gains = g_attn[:, 4 * local_cols : 4 * local_cols + 4]
    return (
        out_full,
        jnp.stack(grad_rows),
        grad_qkv,
        grad_out,
        jnp.stack([g_gate, g_up]),
        g_down.T,
        gains[:, 0] + gains[:, 1],
        gains[:, 2] + gains[:, 3],
    )


def solution(mesh):
    in_specs = (
        P(None, "dp", None),
        P(None, "dp", None),
        P(None, "dp", None),
        P(),
        P(None, None, "tensor"),
        P("tensor", None),
        P(None, None, "tensor"),
        P("tensor", None),
        P(),
        P(),
    )
    out_specs = (
        P(None, "dp", None),
        P(None, "dp", None),
        P(None, "dp", "tensor"),
        P("tensor", "dp"),
        P(None, "dp", "tensor"),
        P("tensor", "dp"),
        P("dp"),
        P("dp"),
    )
    return jax.shard_map(local, mesh=mesh, in_specs=in_specs, out_specs=out_specs, check_vma=False)
```

```python
import functools

import jax
import jax.numpy as jnp
from jax import lax
from jax.experimental import pallas as pl
from jax.experimental.pallas import tpu as pltpu
from jax.sharding import PartitionSpec as P

HEAD_DIM = 64
LANES = 128
F32 = jnp.float32
BF16 = jnp.bfloat16
VMEM = pl.BlockSpec(memory_space=pltpu.VMEM)
SMEM = pl.BlockSpec(memory_space=pltpu.SMEM)


def call(kernel, out_shape, in_specs, scratch=(), flops=0, bytes_accessed=0, name=None):
    return pl.pallas_call(
        kernel,
        out_shape=out_shape,
        in_specs=in_specs,
        out_specs=jax.tree.map(lambda _: VMEM, out_shape),
        scratch_shapes=list(scratch),
        compiler_params=pltpu.CompilerParams(vmem_limit_bytes=56 * 2**20),
        cost_estimate=pl.CostEstimate(
            flops=flops, bytes_accessed=bytes_accessed, transcendentals=0
        ),
        name=name,
    )


def nn(a, b):
    return lax.dot_general(a, b, (((1,), (0,)), ((), ())), preferred_element_type=F32)


def nt(a, b):
    return lax.dot_general(a, b, (((1,), (1,)), ((), ())), preferred_element_type=F32)


def tn(a, b):
    return lax.dot_general(a, b, (((0,), (0,)), ((), ())), preferred_element_type=F32)


def half_at(which, half):
    return pl.ds(pl.multiple_of(which * half, half), half)


def join_into(ref, side, own_ref, other_ref):
    half = own_ref.shape[1]
    ref[:, half_at(side, half)] = own_ref[...]
    ref[:, half_at(1 - side, half)] = other_ref[...]


def tiles(total, step):
    return [(at, min(step, total - at)) for at in range(0, total, step)]


def write_bias(bias_ref, len_ref):
    rows = bias_ref.shape[0]
    at_i = lax.broadcasted_iota(jnp.int32, (rows, rows), 0)
    at_j = lax.broadcasted_iota(jnp.int32, (rows, rows), 1)
    segment_i = jnp.zeros((rows, rows), jnp.int32)
    segment_j = jnp.zeros((rows, rows), jnp.int32)
    end = jnp.int32(0)
    for s in range(len_ref.shape[0]):
        end = end + len_ref[s]
        segment_i = segment_i + (at_i >= end).astype(jnp.int32)
        segment_j = segment_j + (at_j >= end).astype(jnp.int32)
    allowed = (segment_i == segment_j) & (at_j <= at_i)
    bias_ref[...] = jnp.where(allowed, 0.0, -1e30).astype(F32)


def one_head(pair, which):
    lane = lax.broadcasted_iota(jnp.int32, pair.shape, 1)
    keep = lane < HEAD_DIM if which == 0 else lane >= HEAD_DIM
    return jnp.where(keep, pair.astype(F32), 0.0).astype(BF16)


def forward_kernel(
    len_ref, side_ref, own_ref, other_ref, gain_ref, w_ref,
    h_ref, normed_ref, qkv_ref, lse_ref, mixed_ref, inv_ref, bias_ref,
):
    side = side_ref[0]
    join_into(h_ref, side, own_ref, other_ref)
    values = h_ref[...].astype(F32)
    inv = lax.rsqrt(jnp.mean(values * values, axis=-1, keepdims=True) + 1e-05)
    inv_ref[...] = inv
    normed_ref[...] = (values * inv * gain_ref[...]).astype(BF16)
    write_bias(bias_ref, len_ref)
    for c in range(3):
        qkv_ref[c] = nn(normed_ref[...], w_ref[c]).astype(BF16)
    for pair in range(mixed_ref.shape[1] // LANES):
        cols = slice(pair * LANES, (pair + 1) * LANES)
        total = None
        for which in range(2):
            keys = one_head(qkv_ref[1, :, cols], which)
            scores = nt(qkv_ref[0, :, cols], keys) * HEAD_DIM**-0.5 + bias_ref[...]
            row_max = jnp.max(scores, axis=-1, keepdims=True)
            lse = row_max + jnp.log(jnp.sum(jnp.exp(scores - row_max), axis=-1, keepdims=True))
            head = 2 * pair + which
            lse_ref[:, head : head + 1] = lse
            soft = jnp.exp(scores - lse).astype(BF16)
            product = nn(soft, one_head(qkv_ref[2, :, cols], which))
            total = product if total is None else total + product
        mixed_ref[:, cols] = total.astype(BF16)


def ffn_kernel(
    side_ref, h_ref, mixed_ref, mixed_got_ref, w_out_ref, w_out_got_ref, co_ref, co_got_ref,
    gain_ref, w_gu_ref, w_down_ref,
    middle_ref, normed_ref, up_ref, act_ref, d_gate_ref, d_up_ref, d_part_ref, theirs_ref, packed_ref,
):
    side = side_ref[0]
    half = co_ref.shape[1]
    features = h_ref.shape[1]
    join_into(up_ref, side, co_ref, co_got_ref)
    for at, size in tiles(features, 256):
        cols = slice(at, at + size)
        middle_ref[:, cols] = h_ref[:, cols].astype(F32) + (
            nn(mixed_ref[...], w_out_ref[:, cols]) + nn(mixed_got_ref[...], w_out_got_ref[:, cols])
        )
    values = middle_ref[...]
    inv = lax.rsqrt(jnp.mean(values * values, axis=-1, keepdims=True) + 1e-05)
    normed_ref[...] = (values * inv * gain_ref[...]).astype(BF16)
    for at, size in tiles(act_ref.shape[1], 256):
        cols = slice(at, at + size)
        gate = nn(normed_ref[...], w_gu_ref[0, :, cols])
        up = nn(normed_ref[...], w_gu_ref[1, :, cols])
        d_act = nt(up_ref[...], w_down_ref[cols, :])
        sigm = jax.nn.sigmoid(gate)
        silu = gate * sigm
        act_ref[:, cols] = (silu * up).astype(BF16)
        d_gate_ref[:, cols] = (d_act * up * sigm * (1.0 + gate * (1.0 - sigm))).astype(BF16)
        d_up_ref[:, cols] = (d_act * silu).astype(BF16)
    for at, size in tiles(features, 256):
        cols = slice(at, at + size)
        d_part_ref[:, cols] = (
            nt(d_gate_ref[...], w_gu_ref[0, cols, :]) + nt(d_up_ref[...], w_gu_ref[1, cols, :])
        ).astype(BF16)
    theirs_ref[...] = nn(act_ref[...], w_down_ref[:, half_at(1 - side, half)]).astype(BF16)
    packed_ref[...] = middle_ref[:, half_at(side, half)] + nn(
        act_ref[...], w_down_ref[:, half_at(side, half)]
    )


def backward_kernel(
    len_ref, side_ref, part_ref, part_got_ref, middle_ref, up_ref, gain_f_ref, w_out_ref,
    qkv_ref, lse_ref, h_ref, inv_ref, gain_a_ref, w_ref,
    d_attn_ref, d_qkv_ref, d_mid_ref, theirs_ref, mine_ref, stat_ref, sums_ref,
    bias_ref, d_mixed_ref, d_full_ref,
):
    side = side_ref[0]
    half = d_mid_ref.shape[1]
    features = h_ref.shape[1]
    middle = middle_ref[...]
    inv_f = lax.rsqrt(jnp.mean(middle * middle, axis=-1, keepdims=True) + 1e-05)
    d_normed = part_ref[...].astype(F32) + part_got_ref[...].astype(F32)
    scaled = gain_f_ref[...] * d_normed
    d_full_ref[...] = (
        up_ref[...].astype(F32)
        + inv_f * scaled
        - middle * inv_f**3 * jnp.mean(scaled * middle, axis=-1, keepdims=True)
    )
    sums_ref[1:2, :] = jnp.sum(d_normed * middle * inv_f, axis=0, keepdims=True)
    d_attn_ref[...] = d_full_ref[...].astype(BF16)
    d_mid_ref[...] = d_full_ref[:, half_at(side, half)]
    d_mixed_ref[...] = nt(d_attn_ref[...], w_out_ref[...]).astype(BF16)
    write_bias(bias_ref, len_ref)
    for pair in range(d_mixed_ref.shape[1] // LANES):
        cols = slice(pair * LANES, (pair + 1) * LANES)
        d_q, d_k, d_v = [], [], []
        for which in range(2):
            keys = one_head(qkv_ref[1, :, cols], which)
            head = 2 * pair + which
            scores = nt(qkv_ref[0, :, cols], keys) * HEAD_DIM**-0.5 + bias_ref[...]
            soft = jnp.exp(scores - lse_ref[:, head : head + 1])
            d_mixed = one_head(d_mixed_ref[:, cols], which)
            d_probs = nt(d_mixed, qkv_ref[2, :, cols])
            row_dots = jnp.sum(soft * d_probs, axis=-1, keepdims=True)
            d_scores = (soft * (d_probs - row_dots)).astype(BF16)
            d_q.append(nn(d_scores, keys))
            d_k.append(tn(d_scores, one_head(qkv_ref[0, :, cols], which)))
            d_v.append(tn(soft.astype(BF16), d_mixed))
        d_qkv_ref[0, :, cols] = ((d_q[0] + d_q[1]) * HEAD_DIM**-0.5).astype(BF16)
        d_qkv_ref[1, :, cols] = ((d_k[0] + d_k[1]) * HEAD_DIM**-0.5).astype(BF16)
        d_qkv_ref[2, :, cols] = (d_v[0] + d_v[1]).astype(BF16)
    for at, size in tiles(features, 256):
        cols = slice(at, at + size)
        part = nt(d_qkv_ref[0], w_ref[0, cols, :])
        part = part + nt(d_qkv_ref[1], w_ref[1, cols, :])
        d_full_ref[:, cols] = part + nt(d_qkv_ref[2], w_ref[2, cols, :])
    whole = d_full_ref[...]
    weighted = whole * h_ref[...].astype(F32)
    stat_ref[...] = jnp.sum(gain_a_ref[...] * weighted, axis=-1, keepdims=True)
    sums_ref[0:1, :] = jnp.sum(weighted * inv_ref[...], axis=0, keepdims=True)
    mine_ref[...] = d_full_ref[:, half_at(side, half)]
    theirs_ref[...] = d_full_ref[:, half_at(1 - side, half)].astype(BF16)


def reversed_bits(value, bits):
    out = value * 0
    for b in range(bits):
        out = out + (((value >> b) & 1) << (bits - 1 - b))
    return out


def product_kernel(pairs, columns, bits, extra, me_ref, *refs):
    count = 2 * sum(pairs)
    ins = refs[: count + extra]
    send_ref, keep_ref, wide_ref = refs[count + extra :]
    groups = 1 << bits
    rows = wide_ref.shape[0]
    part = rows // groups
    me = me_ref[0]

    def spread(cols):
        size = cols.stop - cols.start
        for place in range(groups):
            source = reversed_bits(me * 0 + place, bits) ^ me ^ (groups - 1)
            block = wide_ref[pl.ds(pl.multiple_of(source * part, part), part), :size].astype(BF16)
            if place < groups // 2:
                send_ref[place * part : (place + 1) * part, cols] = block
            else:
                low = (place - groups // 2) * part
                keep_ref[low : low + part, cols] = block

    at_in, at_out = 0, 0
    for terms, width in zip(pairs, columns):
        group = ins[at_in : at_in + 2 * terms]
        at_in += 2 * terms
        for at, size in tiles(width, 256):
            total = None
            for t in range(terms):
                product = tn(group[2 * t][...], group[2 * t + 1][:, at : at + size])
                total = product if total is None else total + product
            wide_ref[:, :size] = total
            spread(slice(at_out + at, at_out + at + size))
        at_out += width
    if extra:
        width = ins[-1].shape[1]
        wide_ref[:, :width] = ins[-1][...]
        spread(slice(at_out, at_out + width))


def product(terms, groups, me, extra=None, name=None):
    rows = terms[0][0][0].shape[1]
    columns = [block[0][1].shape[1] for block in terms]
    flat = [array for block in terms for pair in block for array in pair]
    total = sum(columns)
    if extra is not None:
        flat.append(extra)
        total += extra.shape[1]
    depth = sum(left.shape[0] for left, _ in terms[0])
    kernel = functools.partial(
        product_kernel,
        [len(block) for block in terms],
        columns,
        groups.bit_length() - 1,
        int(extra is not None),
    )
    out = jax.ShapeDtypeStruct((rows // 2, total), BF16)
    return call(
        kernel,
        (out, out),
        [SMEM] + [VMEM] * len(flat),
        [pltpu.VMEM((rows, 256), F32)],
        flops=2 * rows * depth * total,
        bytes_accessed=2 * rows * total + 2 * depth * (rows + total),
        name=name,
    )(me.reshape(1), *flat)


def halve(send, keep, groups):
    bits = groups.bit_length() - 1
    for b in range(bits):
        got = lax.ppermute(send, "dp", [(j, j ^ (1 << b)) for j in range(groups)])
        if b == bits - 1:
            return keep.astype(F32) + got.astype(F32)
        half = keep.shape[0] // 2
        send = (keep[:half].astype(F32) + got[:half].astype(F32)).astype(BF16)
        keep = (keep[half:].astype(F32) + got[half:].astype(F32)).astype(BF16)


def scatter_rows(whole, groups, me):
    rows, cols = whole.shape
    part = rows // groups
    bits = groups.bit_length() - 1
    split = whole.reshape((2,) * bits + (part, cols))
    current = split.transpose(tuple(range(bits - 1, -1, -1)) + (bits, bits + 1)).reshape(rows, cols)
    current = current.astype(BF16)
    for b in range(bits):
        half = current.shape[0] // 2
        bit = (me >> b) & 1
        send = lax.dynamic_slice_in_dim(current, (1 - bit) * half, half, 0)
        keep = lax.dynamic_slice_in_dim(current, bit * half, half, 0)
        got = lax.ppermute(send, "dp", [(j, j ^ (1 << b)) for j in range(groups)])
        total = keep.astype(F32) + got.astype(F32)
        current = total if b == bits - 1 else total.astype(BF16)
    return current


def reduced(terms, groups, me, extra=None, name=None):
    rows = terms[0][0][0].shape[1]
    if rows // groups % 16 == 0:
        return halve(*product(terms, groups, me, extra, name), groups)
    blocks = [sum(tn(left, right) for left, right in block) for block in terms]
    if extra is not None:
        blocks.append(extra)
    return scatter_rows(jnp.concatenate(blocks, axis=1), groups, me)


def routes(dealing, groups, me):
    micros, total = dealing.shape
    blocks = dealing // groups
    spots = jnp.arange(groups)
    mine = lax.dynamic_slice_in_dim(blocks, me * groups, groups, axis=1)
    earlier = (mine[:, None, :] == mine[:, :, None]) & (spots[None, None, :] < spots[None, :, None])
    mine_slots = mine * 2 + jnp.sum(earlier.astype(jnp.int32), axis=2)
    arrivals = jnp.arange(total)
    hits = dealing[:, None, :] == (me * groups + spots)[None, :, None]
    source = jnp.sum(jnp.where(hits, arrivals[None, None, :], 0), axis=2)
    ahead = (
        (blocks[:, None, :] == me)
        & (arrivals[None, None, :] // groups == source[:, :, None] // groups)
        & (arrivals[None, None, :] < source[:, :, None])
    )
    recv_slots = source // groups * 2 + jnp.sum(ahead.astype(jnp.int32), axis=2)
    return mine_slots, recv_slots


def chosen_of(slots, groups):
    matches = slots[:, None, :] == jnp.arange(2 * groups)[None, :, None]
    return jnp.sum(jnp.where(matches, jnp.arange(groups)[None, None, :], 0), axis=2)


def rows_at(array, index):
    return array.at[index].get(mode="promise_in_bounds")


def deal(pieces, chosen, take_slots):
    count, rows, cols = pieces.shape
    send = rows_at(pieces, chosen).reshape(count, 2, rows, cols)
    got = lax.all_to_all(send, "dp", 0, 0, tiled=True).reshape(count * 2, rows, cols)
    return rows_at(got, take_slots).reshape(count * rows, cols)


def swap(array):
    return lax.ppermute(array, "tensor", [(0, 1), (1, 0)])


def joined(own, other, side, axis):
    first = jnp.where(side == 0, own, other)
    second = jnp.where(side == 0, other, own)
    return jnp.concatenate([first, second], axis=axis)


def local(
    inputs, cotangent, lengths, dealing, w_qkv, w_out, w_gate_up, w_down, gain_attn, gain_ffn
):
    groups = lax.axis_size("dp")
    me = lax.axis_index("dp")
    side = lax.axis_index("tensor")
    micros, rows, features = inputs.shape
    piece_rows = rows // groups
    half = features // 2
    cols = w_out.shape[0]
    hidden = w_down.shape[0]
    heads = cols // HEAD_DIM
    side_arg = side.reshape(1)
    gain_a = gain_attn.reshape(1, features)
    gain_f = gain_ffn.reshape(1, features)

    mine_slots, recv_slots = routes(dealing, groups, me)
    chosen_out = chosen_of(mine_slots, groups)
    chosen_back = chosen_of(recv_slots, groups)

    def half_of(array):
        return lax.dynamic_slice_in_dim(array, side * half, half, axis=-1)

    def shape_of(*dims, dtype=BF16):
        return jax.ShapeDtypeStruct(dims, dtype)

    def bring(array, m):
        pieces = half_of(array[m]).reshape(groups, piece_rows, half)
        return deal(pieces, chosen_out[m], recv_slots[m])

    def home(array, m):
        return deal(array.reshape(groups, piece_rows, half), chosen_back[m], mine_slots[m])

    in_half = [bring(inputs, m) for m in range(micros)]
    co_half = [bring(cotangent, m) for m in range(micros)]
    w_out_got = swap(w_out)

    forward = call(
        forward_kernel,
        (
            shape_of(rows, features), shape_of(rows, features), shape_of(3, rows, cols),
            shape_of(rows, heads, dtype=F32), shape_of(rows, cols), shape_of(rows, 1, dtype=F32),
        ),
        [SMEM, SMEM] + [VMEM] * 4,
        [pltpu.VMEM((rows, rows), F32)],
        flops=2 * rows * (features * 3 * cols + 2 * rows * cols * 2),
        bytes_accessed=2 * (3 * features * cols + rows * (3 * features + 4 * cols)),
        name="attention_forward",
    )
    kept = []
    for m in range(micros):
        other = swap(in_half[m])
        kept.append(forward(lengths[m, 0], side_arg, in_half[m], other, gain_a, w_qkv))

    ffn_call = call(
        ffn_kernel,
        (
            shape_of(rows, features, dtype=F32), shape_of(rows, features), shape_of(rows, features),
            shape_of(rows, hidden), shape_of(rows, hidden), shape_of(rows, hidden),
            shape_of(rows, features), shape_of(rows, half), shape_of(rows, half, dtype=F32),
        ),
        [SMEM] + [VMEM] * 10,
        flops=2 * rows * features * (6 * hidden + 2 * cols),
        bytes_accessed=2 * (3 * features * hidden + 2 * features * cols + rows * (8 * features + 3 * hidden)),
        name="feed_forward",
    )
    ffn = []
    for m in range(micros):
        h, mixed = kept[m][0], kept[m][4]
        ffn.append(
            ffn_call(
                side_arg, h, mixed, swap(mixed), w_out, w_out_got, co_half[m], swap(co_half[m]),
                gain_f, w_gate_up, w_down,
            )
        )
    d_got = [swap(ffn[m][6]) for m in range(micros)]

    g_down = reduced([[(f[2], f[3]) for f in ffn]], groups, me, name="grad_down")
    g_gate = reduced([[(f[1], f[4]) for f in ffn]], groups, me, name="grad_gate")
    g_up = reduced([[(f[1], f[5]) for f in ffn]], groups, me, name="grad_up")

    out_full = []
    for m in range(micros):
        packed = (ffn[m][8] + swap(ffn[m][7]).astype(F32)).astype(BF16)
        back = home(packed, m)
        out_full.append(joined(back, swap(back), side, 1))

    backward = call(
        backward_kernel,
        (
            shape_of(rows, features), shape_of(3, rows, cols), shape_of(rows, half, dtype=F32),
            shape_of(rows, half), shape_of(rows, half, dtype=F32), shape_of(rows, 1, dtype=F32),
            shape_of(2, features, dtype=F32),
        ),
        [SMEM, SMEM] + [VMEM] * 12,
        [
            pltpu.VMEM((rows, rows), F32),
            pltpu.VMEM((rows, cols), BF16),
            pltpu.VMEM((rows, features), F32),
        ],
        flops=2 * rows * (features * 4 * cols + 2 * rows * cols * 5),
        bytes_accessed=2 * (4 * features * cols + rows * (8 * features + 9 * cols)),
        name="attention_backward",
    )
    tail = []
    for m in range(micros):
        h, normed, qkv, lse, mixed, inv = kept[m]
        tail.append(
            backward(
                lengths[m, 0], side_arg, ffn[m][6], d_got[m], ffn[m][0], ffn[m][2], gain_f, w_out,
                qkv, lse, h, inv, gain_a, w_qkv,
            )
        )
    grad_rows = []
    gain_half = half_of(gain_a)
    for m in range(micros):
        d_mid, theirs, mine, stat = tail[m][2:6]
        inv = kept[m][5]
        d_normed = mine + swap(theirs).astype(F32)
        mean = (stat + swap(stat)) / features
        d_hidden = d_mid + inv * (gain_half * d_normed) - in_half[m].astype(F32) * inv**3 * mean
        back = home(d_hidden.astype(BF16), m)
        grad_rows.append(joined(back, swap(back), side, 1))

    sums = sum(item[6] for item in tail)
    extra = jnp.pad(sums.T, ((0, 0), (0, LANES - 2)))
    g_attn = reduced(
        [
            [(kept[m][1], tail[m][1][0]) for m in range(micros)],
            [(kept[m][1], tail[m][1][1]) for m in range(micros)],
            [(kept[m][1], tail[m][1][2]) for m in range(micros)],
            [(tail[m][0], kept[m][4]) for m in range(micros)],
        ],
        groups,
        me,
        extra,
        name="grad_attention",
    )
    grad_qkv = jnp.stack([g_attn[:, c * cols : (c + 1) * cols] for c in range(3)])
    grad_out = g_attn[:, 3 * cols : 4 * cols].T
    gains = g_attn[:, 4 * cols : 4 * cols + 2]
    gains = gains + swap(gains)
    return (
        jnp.stack(out_full),
        jnp.stack(grad_rows),
        grad_qkv,
        grad_out,
        jnp.stack([g_gate, g_up]),
        g_down.T,
        gains[:, 0],
        0.5 * gains[:, 1],
    )


def solution(mesh):
    in_specs = (
        P(None, "dp", None),
        P(None, "dp", None),
        P(None, "dp", None),
        P(),
        P(None, None, "tensor"),
        P("tensor", None),
        P(None, None, "tensor"),
        P("tensor", None),
        P(),
        P(),
    )
    out_specs = (
        P(None, "dp", None),
        P(None, "dp", None),
        P(None, "dp", "tensor"),
        P("tensor", "dp"),
        P(None, "dp", "tensor"),
        P("tensor", "dp"),
        P("dp"),
        P("dp"),
    )
    return jax.shard_map(local, mesh=mesh, in_specs=in_specs, out_specs=out_specs, check_vma=False)
```

```python
import functools

import jax
import jax.numpy as jnp
from jax import lax
from jax.experimental import pallas as pl
from jax.experimental.pallas import tpu as pltpu
from jax.sharding import PartitionSpec as P

HEAD_DIM = 64
LANES = 128
F32 = jnp.float32
BF16 = jnp.bfloat16
VMEM = pl.BlockSpec(memory_space=pltpu.VMEM)
SMEM = pl.BlockSpec(memory_space=pltpu.SMEM)


def call(kernel, out_shape, in_specs, scratch=(), flops=0, bytes_accessed=0):
    return pl.pallas_call(
        kernel,
        out_shape=out_shape,
        in_specs=in_specs,
        out_specs=jax.tree.map(lambda _: VMEM, out_shape),
        scratch_shapes=list(scratch),
        compiler_params=pltpu.CompilerParams(vmem_limit_bytes=56 * 2**20),
        cost_estimate=pl.CostEstimate(
            flops=flops, bytes_accessed=bytes_accessed, transcendentals=0
        ),
    )


def nn(a, b):
    return lax.dot_general(a, b, (((1,), (0,)), ((), ())), preferred_element_type=F32)


def nt(a, b):
    return lax.dot_general(a, b, (((1,), (1,)), ((), ())), preferred_element_type=F32)


def tn(a, b):
    return lax.dot_general(a, b, (((0,), (0,)), ((), ())), preferred_element_type=F32)


def half_at(which, half):
    return pl.ds(pl.multiple_of(which * half, half), half)


def join_into(ref, side, own_ref, other_ref):
    half = own_ref.shape[1]
    ref[:, half_at(side, half)] = own_ref[...]
    ref[:, half_at(1 - side, half)] = other_ref[...]


def tiles(total, step):
    return [(at, min(step, total - at)) for at in range(0, total, step)]


def write_bias(bias_ref, len_ref):
    rows = bias_ref.shape[0]
    at_i = lax.broadcasted_iota(jnp.int32, (rows, rows), 0)
    at_j = lax.broadcasted_iota(jnp.int32, (rows, rows), 1)
    segment_i = jnp.zeros((rows, rows), jnp.int32)
    segment_j = jnp.zeros((rows, rows), jnp.int32)
    end = jnp.int32(0)
    for s in range(len_ref.shape[0]):
        end = end + len_ref[s]
        segment_i = segment_i + (at_i >= end).astype(jnp.int32)
        segment_j = segment_j + (at_j >= end).astype(jnp.int32)
    allowed = (segment_i == segment_j) & (at_j <= at_i)
    bias_ref[...] = jnp.where(allowed, 0.0, -1e30).astype(F32)


def one_head(pair, which):
    lane = lax.broadcasted_iota(jnp.int32, pair.shape, 1)
    keep = lane < HEAD_DIM if which == 0 else lane >= HEAD_DIM
    return jnp.where(keep, pair.astype(F32), 0.0).astype(BF16)


def forward_kernel(
    len_ref, side_ref, own_ref, other_ref, gain_ref, w_ref,
    h_ref, normed_ref, qkv_ref, lse_ref, mixed_ref, inv_ref, bias_ref,
):
    side = side_ref[0]
    join_into(h_ref, side, own_ref, other_ref)
    values = h_ref[...].astype(F32)
    inv = lax.rsqrt(jnp.mean(values * values, axis=-1, keepdims=True) + 1e-05)
    inv_ref[...] = inv
    normed_ref[...] = (values * inv * gain_ref[...]).astype(BF16)
    write_bias(bias_ref, len_ref)
    for c in range(3):
        qkv_ref[c] = nn(normed_ref[...], w_ref[c]).astype(BF16)
    for pair in range(mixed_ref.shape[1] // LANES):
        cols = slice(pair * LANES, (pair + 1) * LANES)
        total = None
        for which in range(2):
            keys = one_head(qkv_ref[1, :, cols], which)
            scores = nt(qkv_ref[0, :, cols], keys) * HEAD_DIM**-0.5 + bias_ref[...]
            row_max = jnp.max(scores, axis=-1, keepdims=True)
            lse = row_max + jnp.log(jnp.sum(jnp.exp(scores - row_max), axis=-1, keepdims=True))
            head = 2 * pair + which
            lse_ref[:, head : head + 1] = lse
            soft = jnp.exp(scores - lse).astype(BF16)
            product = nn(soft, one_head(qkv_ref[2, :, cols], which))
            total = product if total is None else total + product
        mixed_ref[:, cols] = total.astype(BF16)


def ffn_forward_kernel(
    side_ref, h_ref, mixed_ref, mixed_got_ref, w_out_ref, w_out_got_ref, gain_ref, w_gu_ref, w_down_ref,
    middle_ref, normed_ref, gate_ref, up_ref, act_ref, theirs_ref, packed_ref,
):
    side = side_ref[0]
    half = packed_ref.shape[1]
    features = h_ref.shape[1]
    for at, size in tiles(features, 256):
        cols = slice(at, at + size)
        middle_ref[:, cols] = h_ref[:, cols].astype(F32) + (
            nn(mixed_ref[...], w_out_ref[:, cols]) + nn(mixed_got_ref[...], w_out_got_ref[:, cols])
        )
    values = middle_ref[...]
    inv = lax.rsqrt(jnp.mean(values * values, axis=-1, keepdims=True) + 1e-05)
    normed_ref[...] = (values * inv * gain_ref[...]).astype(BF16)
    for at, size in tiles(act_ref.shape[1], 256):
        cols = slice(at, at + size)
        gate = nn(normed_ref[...], w_gu_ref[0, :, cols])
        up = nn(normed_ref[...], w_gu_ref[1, :, cols])
        gate_ref[:, cols] = gate
        up_ref[:, cols] = up
        act_ref[:, cols] = (gate * jax.nn.sigmoid(gate) * up).astype(BF16)
    theirs_ref[...] = nn(act_ref[...], w_down_ref[:, half_at(1 - side, half)]).astype(BF16)
    packed_ref[...] = middle_ref[:, half_at(side, half)] + nn(
        act_ref[...], w_down_ref[:, half_at(side, half)]
    )


def ffn_backward_kernel(
    side_ref, co_ref, co_got_ref, gate_ref, up_ref, w_gu_ref, w_down_ref,
    upstream_ref, d_gate_ref, d_up_ref, d_part_ref,
):
    join_into(upstream_ref, side_ref[0], co_ref, co_got_ref)
    for at, size in tiles(gate_ref.shape[1], 256):
        cols = slice(at, at + size)
        d_act = nt(upstream_ref[...], w_down_ref[cols, :])
        gate = gate_ref[:, cols]
        sigm = jax.nn.sigmoid(gate)
        d_gate_ref[:, cols] = (
            d_act * up_ref[:, cols] * sigm * (1.0 + gate * (1.0 - sigm))
        ).astype(BF16)
        d_up_ref[:, cols] = (d_act * (gate * sigm)).astype(BF16)
    for at, size in tiles(d_part_ref.shape[1], 256):
        cols = slice(at, at + size)
        d_part_ref[:, cols] = (
            nt(d_gate_ref[...], w_gu_ref[0, cols, :]) + nt(d_up_ref[...], w_gu_ref[1, cols, :])
        ).astype(BF16)


def backward_kernel(
    len_ref, side_ref, part_ref, part_got_ref, middle_ref, up_ref, gain_f_ref, w_out_ref,
    qkv_ref, lse_ref, h_ref, inv_ref, gain_a_ref, w_ref,
    d_attn_ref, d_qkv_ref, d_mid_ref, theirs_ref, mine_ref, stat_ref, sums_ref,
    bias_ref, d_mixed_ref, d_full_ref,
):
    side = side_ref[0]
    half = d_mid_ref.shape[1]
    features = h_ref.shape[1]
    middle = middle_ref[...]
    inv_f = lax.rsqrt(jnp.mean(middle * middle, axis=-1, keepdims=True) + 1e-05)
    d_normed = part_ref[...].astype(F32) + part_got_ref[...].astype(F32)
    scaled = gain_f_ref[...] * d_normed
    d_full_ref[...] = (
        up_ref[...].astype(F32)
        + inv_f * scaled
        - middle * inv_f**3 * jnp.mean(scaled * middle, axis=-1, keepdims=True)
    )
    sums_ref[1:2, :] = jnp.sum(d_normed * middle * inv_f, axis=0, keepdims=True)
    d_attn_ref[...] = d_full_ref[...].astype(BF16)
    d_mid_ref[...] = d_full_ref[:, half_at(side, half)]
    d_mixed_ref[...] = nt(d_attn_ref[...], w_out_ref[...]).astype(BF16)
    write_bias(bias_ref, len_ref)
    for pair in range(d_mixed_ref.shape[1] // LANES):
        cols = slice(pair * LANES, (pair + 1) * LANES)
        d_q, d_k, d_v = [], [], []
        for which in range(2):
            keys = one_head(qkv_ref[1, :, cols], which)
            head = 2 * pair + which
            scores = nt(qkv_ref[0, :, cols], keys) * HEAD_DIM**-0.5 + bias_ref[...]
            soft = jnp.exp(scores - lse_ref[:, head : head + 1])
            d_mixed = one_head(d_mixed_ref[:, cols], which)
            d_probs = nt(d_mixed, qkv_ref[2, :, cols])
            row_dots = jnp.sum(soft * d_probs, axis=-1, keepdims=True)
            d_scores = (soft * (d_probs - row_dots)).astype(BF16)
            d_q.append(nn(d_scores, keys))
            d_k.append(tn(d_scores, one_head(qkv_ref[0, :, cols], which)))
            d_v.append(tn(soft.astype(BF16), d_mixed))
        d_qkv_ref[0, :, cols] = ((d_q[0] + d_q[1]) * HEAD_DIM**-0.5).astype(BF16)
        d_qkv_ref[1, :, cols] = ((d_k[0] + d_k[1]) * HEAD_DIM**-0.5).astype(BF16)
        d_qkv_ref[2, :, cols] = (d_v[0] + d_v[1]).astype(BF16)
    for at, size in tiles(features, 256):
        cols = slice(at, at + size)
        part = nt(d_qkv_ref[0], w_ref[0, cols, :])
        part = part + nt(d_qkv_ref[1], w_ref[1, cols, :])
        d_full_ref[:, cols] = part + nt(d_qkv_ref[2], w_ref[2, cols, :])
    whole = d_full_ref[...]
    weighted = whole * h_ref[...].astype(F32)
    stat_ref[...] = jnp.sum(gain_a_ref[...] * weighted, axis=-1, keepdims=True)
    sums_ref[0:1, :] = jnp.sum(weighted * inv_ref[...], axis=0, keepdims=True)
    mine_ref[...] = d_full_ref[:, half_at(side, half)]
    theirs_ref[...] = d_full_ref[:, half_at(1 - side, half)].astype(BF16)


def reversed_bits(value, bits):
    out = value * 0
    for b in range(bits):
        out = out + (((value >> b) & 1) << (bits - 1 - b))
    return out


def product_kernel(pairs, columns, bits, extra, halves, place_ref, *refs):
    count = sum(pairs) * (3 if halves else 2)
    ins = refs[: count + extra]
    send_ref, keep_ref, wide_ref = refs[count + extra :]
    groups = 1 << bits
    rows = wide_ref.shape[0]
    part = rows // groups
    me, side = place_ref[0], place_ref[1]

    def spread(cols):
        size = cols.stop - cols.start
        for place in range(groups):
            source = reversed_bits(me * 0 + place, bits) ^ me ^ (groups - 1)
            block = wide_ref[pl.ds(pl.multiple_of(source * part, part), part), :size].astype(BF16)
            if place < groups // 2:
                send_ref[place * part : (place + 1) * part, cols] = block
            else:
                low = (place - groups // 2) * part
                keep_ref[low : low + part, cols] = block

    at_in, at_out = 0, 0
    for terms, width in zip(pairs, columns):
        stride = 3 if halves else 2
        group = ins[at_in : at_in + stride * terms]
        at_in += stride * terms
        for at, size in tiles(width, 256):
            for which in range(stride - 1):
                total = None
                for t in range(terms):
                    term = group[stride * t : stride * t + stride]
                    product = tn(term[which][...], term[-1][:, at : at + size])
                    total = product if total is None else total + product
                if halves:
                    wide_ref[half_at(side if which == 0 else 1 - side, rows // 2), :size] = total
                else:
                    wide_ref[:, :size] = total
            spread(slice(at_out + at, at_out + at + size))
        at_out += width
    if extra:
        width = ins[-1].shape[1]
        wide_ref[:, :width] = ins[-1][...]
        spread(slice(at_out, at_out + width))


def product(terms, groups, place, extra=None):
    halves = len(terms[0][0]) == 3
    rows = sum(left.shape[1] for left in terms[0][0][:-1])
    columns = [block[0][-1].shape[1] for block in terms]
    flat = [array for block in terms for pair in block for array in pair]
    total = sum(columns)
    if extra is not None:
        flat.append(extra)
        total += extra.shape[1]
    depth = sum(pair[0].shape[0] for pair in terms[0])
    kernel = functools.partial(
        product_kernel,
        [len(block) for block in terms],
        columns,
        groups.bit_length() - 1,
        int(extra is not None),
        halves,
    )
    out = jax.ShapeDtypeStruct((rows // 2, total), BF16)
    return call(
        kernel,
        (out, out),
        [SMEM] + [VMEM] * len(flat),
        [pltpu.VMEM((rows, 256), F32)],
        flops=2 * rows * depth * total,
        bytes_accessed=2 * rows * total + 2 * depth * (rows + total),
    )(place, *flat)


def halve(send, keep, groups):
    bits = groups.bit_length() - 1
    for b in range(bits):
        got = lax.ppermute(send, "dp", [(j, j ^ (1 << b)) for j in range(groups)])
        if b == bits - 1:
            return keep.astype(F32) + got.astype(F32)
        half = keep.shape[0] // 2
        send = (keep[:half].astype(F32) + got[:half].astype(F32)).astype(BF16)
        keep = (keep[half:].astype(F32) + got[half:].astype(F32)).astype(BF16)


def scatter_rows(whole, groups, me):
    rows, cols = whole.shape
    part = rows // groups
    bits = groups.bit_length() - 1
    split = whole.reshape((2,) * bits + (part, cols))
    current = split.transpose(tuple(range(bits - 1, -1, -1)) + (bits, bits + 1)).reshape(rows, cols)
    current = current.astype(BF16)
    for b in range(bits):
        half = current.shape[0] // 2
        bit = (me >> b) & 1
        send = lax.dynamic_slice_in_dim(current, (1 - bit) * half, half, 0)
        keep = lax.dynamic_slice_in_dim(current, bit * half, half, 0)
        got = lax.ppermute(send, "dp", [(j, j ^ (1 << b)) for j in range(groups)])
        total = keep.astype(F32) + got.astype(F32)
        current = total if b == bits - 1 else total.astype(BF16)
    return current


def reduced(terms, groups, place, extra=None):
    first = terms[0][0]
    rows = sum(left.shape[1] for left in first[:-1])
    if rows // groups % 16 == 0:
        send, keep = product(terms, groups, place, extra)
        return halve(send, keep, groups)

    def left_of(pair):
        return pair[0] if len(pair) == 2 else joined(pair[0], pair[1], place[1], 1)

    blocks = [sum(tn(left_of(pair), pair[-1]) for pair in block) for block in terms]
    if extra is not None:
        blocks.append(extra)
    return scatter_rows(jnp.concatenate(blocks, axis=1), groups, place[0])


def routes(dealing, groups, me):
    _, total = dealing.shape
    blocks = dealing // groups
    spots = jnp.arange(groups)
    mine = lax.dynamic_slice_in_dim(blocks, me * groups, groups, axis=1)
    earlier = (mine[:, None, :] == mine[:, :, None]) & (spots[None, None, :] < spots[None, :, None])
    mine_slots = mine * 2 + jnp.sum(earlier.astype(jnp.int32), axis=2)
    arrivals = jnp.arange(total)
    hits = dealing[:, None, :] == (me * groups + spots)[None, :, None]
    source = jnp.sum(jnp.where(hits, arrivals[None, None, :], 0), axis=2)
    ahead = (
        (blocks[:, None, :] == me)
        & (arrivals[None, None, :] // groups == source[:, :, None] // groups)
        & (arrivals[None, None, :] < source[:, :, None])
    )
    recv_slots = source // groups * 2 + jnp.sum(ahead.astype(jnp.int32), axis=2)
    return mine_slots, recv_slots


def chosen_of(slots, groups):
    matches = slots[:, None, :] == jnp.arange(2 * groups)[None, :, None]
    return jnp.sum(jnp.where(matches, jnp.arange(groups)[None, None, :], 0), axis=2)


def rows_at(array, index):
    return array.at[index].get(mode="promise_in_bounds")


def deal(pieces, chosen, take_slots):
    micros, count, rows, cols = pieces.shape
    index = (chosen + jnp.arange(micros)[:, None] * count).reshape(micros, count, 2)
    index = index.transpose(1, 0, 2).reshape(-1)
    send = rows_at(pieces.reshape(micros * count, rows, cols), index)
    send = send.reshape(count, micros * 2, rows, cols)
    got = lax.all_to_all(send, "dp", 0, 0, tiled=True)
    got = got.reshape(count * micros * 2, rows, cols)
    place = take_slots // 2 * (2 * micros) + take_slots % 2 + jnp.arange(micros)[:, None] * 2
    return [rows_at(got, place[m]).reshape(count * rows, cols) for m in range(micros)]


def swap(array):
    return lax.ppermute(array, "tensor", [(0, 1), (1, 0)])


def joined(own, other, side, axis):
    first = jnp.where(side == 0, own, other)
    second = jnp.where(side == 0, other, own)
    return jnp.concatenate([first, second], axis=axis)


def layer(
    inputs, cotangent, lengths, dealing, w_qkv, w_out, w_gate_up, w_down, gain_attn, gain_ffn
):
    groups = lax.axis_size("dp")
    me = lax.axis_index("dp")
    side = lax.axis_index("tensor")
    micros, rows, features = inputs.shape
    piece_rows = rows // groups
    half = features // 2
    cols = w_out.shape[0]
    hidden = w_down.shape[0]
    heads = cols // HEAD_DIM
    side_arg = side.reshape(1)
    gain_a = gain_attn.reshape(1, features)
    gain_f = gain_ffn.reshape(1, features)

    mine_slots, recv_slots = routes(dealing, groups, me)
    chosen_out = chosen_of(mine_slots, groups)
    chosen_back = chosen_of(recv_slots, groups)

    def half_of(array):
        return lax.dynamic_slice_in_dim(array, side * half, half, axis=-1)

    def shape_of(*dims, dtype=BF16):
        return jax.ShapeDtypeStruct(dims, dtype)

    def home(items, first):
        last = first + len(items)
        pieces = jnp.stack(items).reshape(len(items), groups, piece_rows, half)
        backs = deal(pieces, chosen_back[first:last], mine_slots[first:last])
        return [joined(back, swap(back), side, 1) for back in backs]

    def bring(array):
        pieces = half_of(array).reshape(micros, groups, piece_rows, half)
        return deal(pieces, chosen_out, recv_slots)

    place = jnp.stack([me, side])
    in_half = bring(inputs)
    co_half = bring(cotangent)
    w_out_got = swap(w_out)

    forward = call(
        forward_kernel,
        (
            shape_of(rows, features), shape_of(rows, features), shape_of(3, rows, cols),
            shape_of(rows, heads, dtype=F32), shape_of(rows, cols), shape_of(rows, 1, dtype=F32),
        ),
        [SMEM, SMEM] + [VMEM] * 4,
        [pltpu.VMEM((rows, rows), F32)],
        flops=2 * rows * (features * 3 * cols + 2 * rows * cols * 2),
        bytes_accessed=2 * (3 * features * cols + rows * (3 * features + 4 * cols)),
    )
    kept = []
    for m in range(micros):
        other = swap(in_half[m])
        kept.append(forward(lengths[m, 0], side_arg, in_half[m], other, gain_a, w_qkv))

    ffn_forward = call(
        ffn_forward_kernel,
        (
            shape_of(rows, features, dtype=F32), shape_of(rows, features),
            shape_of(rows, hidden, dtype=F32), shape_of(rows, hidden, dtype=F32), shape_of(rows, hidden),
            shape_of(rows, half), shape_of(rows, half, dtype=F32),
        ),
        [SMEM] + [VMEM] * 8,
        flops=2 * rows * features * (3 * hidden + 2 * cols),
        bytes_accessed=2 * (3 * features * hidden + 2 * features * cols + rows * (6 * features + 5 * hidden)),
    )
    fwd = []
    for m in range(micros):
        h, mixed = kept[m][0], kept[m][4]
        mixed_got = swap(mixed)
        fwd.append(
            ffn_forward(side_arg, h, mixed, mixed_got, w_out, w_out_got, gain_f, w_gate_up, w_down)
        )
    packed = [(fwd[m][6] + swap(fwd[m][5]).astype(F32)).astype(BF16) for m in range(micros)]
    out_full = home(packed, 0)

    ffn_backward = call(
        ffn_backward_kernel,
        (
            shape_of(rows, features), shape_of(rows, hidden), shape_of(rows, hidden),
            shape_of(rows, features),
        ),
        [SMEM] + [VMEM] * 6,
        flops=2 * rows * features * 3 * hidden,
        bytes_accessed=2 * (3 * features * hidden + rows * (3 * features + 6 * hidden)),
    )
    co_got = [swap(co_half[m]) for m in range(micros)]
    g_down = reduced([[(co_half[m], co_got[m], fwd[m][4]) for m in range(micros)]], groups, place)
    bwd = []
    for m in range(micros):
        bwd.append(
            ffn_backward(side_arg, co_half[m], co_got[m], fwd[m][2], fwd[m][3], w_gate_up, w_down)
        )
    d_got = [swap(bwd[m][3]) for m in range(micros)]
    g_gate = reduced([[(fwd[m][1], bwd[m][1]) for m in range(micros)]], groups, place)
    g_up = reduced([[(fwd[m][1], bwd[m][2]) for m in range(micros)]], groups, place)

    backward = call(
        backward_kernel,
        (
            shape_of(rows, features), shape_of(3, rows, cols), shape_of(rows, half, dtype=F32),
            shape_of(rows, half), shape_of(rows, half, dtype=F32), shape_of(rows, 1, dtype=F32),
            shape_of(2, features, dtype=F32),
        ),
        [SMEM, SMEM] + [VMEM] * 12,
        [
            pltpu.VMEM((rows, rows), F32),
            pltpu.VMEM((rows, cols), BF16),
            pltpu.VMEM((rows, features), F32),
        ],
        flops=2 * rows * (features * 4 * cols + 2 * rows * cols * 5),
        bytes_accessed=2 * (4 * features * cols + rows * (8 * features + 9 * cols)),
    )
    tail = []
    for m in range(micros):
        h, _, qkv, lse, mixed, inv = kept[m]
        tail.append(
            backward(
                lengths[m, 0], side_arg, bwd[m][3], d_got[m], fwd[m][0], bwd[m][0], gain_f, w_out,
                qkv, lse, h, inv, gain_a, w_qkv,
            )
        )
    grad_rows = []
    gain_half = half_of(gain_a)
    for m in range(micros):
        d_mid, theirs, mine, stat = tail[m][2:6]
        inv = kept[m][5]
        d_normed = mine + swap(theirs).astype(F32)
        mean = (stat + swap(stat)) / features
        d_hidden = d_mid + inv * (gain_half * d_normed) - in_half[m].astype(F32) * inv**3 * mean
        grad_rows += home([d_hidden.astype(BF16)], m)

    sums = sum(item[6] for item in tail)
    extra = jnp.pad(sums.T, ((0, 0), (0, LANES - 2)))
    g_attn = reduced(
        [[(kept[m][1], tail[m][1][c]) for m in range(micros)] for c in range(3)]
        + [[(tail[m][0], kept[m][4]) for m in range(micros)]],
        groups,
        place,
        extra,
    )
    grad_qkv = jnp.stack([g_attn[:, c * cols : (c + 1) * cols] for c in range(3)])
    grad_out = g_attn[:, 3 * cols : 4 * cols].T
    gains = g_attn[:, 4 * cols : 4 * cols + 2]
    gains = gains + swap(gains)
    return (
        jnp.stack(out_full),
        jnp.stack(grad_rows),
        grad_qkv,
        grad_out,
        jnp.stack([g_gate, g_up]),
        g_down.T,
        gains[:, 0],
        0.5 * gains[:, 1],
    )


def solution(mesh):
    in_specs = (
        P(None, "dp", None),
        P(None, "dp", None),
        P(None, "dp", None),
        P(),
        P(None, None, "tensor"),
        P("tensor", None),
        P(None, None, "tensor"),
        P("tensor", None),
        P(),
        P(),
    )
    out_specs = (
        P(None, "dp", None),
        P(None, "dp", None),
        P(None, "dp", "tensor"),
        P("tensor", "dp"),
        P(None, "dp", "tensor"),
        P("tensor", "dp"),
        P("dp"),
        P("dp"),
    )
    return jax.shard_map(layer, mesh=mesh, in_specs=in_specs, out_specs=out_specs, check_vma=False)
```

```python
import functools

import jax
import jax.numpy as jnp
from jax import lax
from jax.experimental import pallas as pl
from jax.experimental.pallas import tpu as pltpu
from jax.sharding import PartitionSpec as P


HEAD_DIM = 64
LANES = 128
F32 = jnp.float32
BF16 = jnp.bfloat16
VMEM = pl.BlockSpec(memory_space=pltpu.VMEM)
SMEM = pl.BlockSpec(memory_space=pltpu.SMEM)
HBM = pl.BlockSpec(memory_space=pltpu.HBM)


class Flow:
    def __init__(self, ins, outs):
        self.ins, self.outs, self.sent = ins, outs, []
        self.begun = set()

    def begin(self, *which):
        for i in which:
            self.ins[i].start()
            self.begun.add(i)

    def need(self, *which):
        self.begin(*[i for i in which if i not in self.begun])
        for i in which:
            self.ins[i].wait()

    def send(self, *which):
        for i in which:
            self.outs[i].start()
            self.sent.append(i)

    def finish(self):
        self.send(*[i for i in self.outs if i not in self.sent])
        for i in self.sent:
            self.outs[i].wait()


def call(
    kernel, out_shape, in_specs, scratch=(), flops=0, bytes_accessed=0,
    hbm_in=(), hbm_out=(), flow=False,
):
    single = not isinstance(out_shape, tuple)
    outs = (out_shape,) if single else out_shape
    n_in, n_out, n_scratch = len(in_specs), len(outs), len(scratch)
    hbm_in = dict(hbm_in)
    specs = [HBM if i in hbm_in else spec for i, spec in enumerate(in_specs)]
    buffers = [pltpu.VMEM(v.shape, v.dtype) for v in hbm_in.values()]
    buffers += [pltpu.VMEM(outs[i].shape, outs[i].dtype) for i in hbm_out]
    semaphores = [pltpu.SemaphoreType.DMA] * len(buffers)

    def staged(*refs):
        refs = list(refs)
        places = list(hbm_in) + [n_in + i for i in hbm_out]
        extra = refs[n_in + n_out + n_scratch :]
        ins, results = {}, {}
        for k, at in enumerate(places):
            buffer, semaphore = extra[k], extra[len(places) + k]
            if at < n_in:
                ins[at] = pltpu.make_async_copy(refs[at], buffer, semaphore)
            else:
                results[at - n_in] = pltpu.make_async_copy(buffer, refs[at], semaphore)
            refs[at] = buffer
        moves = Flow(ins, results)
        if flow:
            kernel(moves, *refs[: n_in + n_out + n_scratch])
        else:
            moves.begin(*ins)
            moves.need(*ins)
            kernel(*refs[: n_in + n_out + n_scratch])
        moves.finish()

    out_specs = tuple(HBM if i in hbm_out else VMEM for i in range(n_out))
    shapes = tuple(
        pltpu.HBM(out.shape, out.dtype) if i in hbm_out else out for i, out in enumerate(outs)
    )
    made = pl.pallas_call(
        staged,
        out_shape=shapes[0] if single else shapes,
        in_specs=specs,
        out_specs=out_specs[0] if single else out_specs,
        scratch_shapes=list(scratch) + buffers + semaphores,
        compiler_params=pltpu.CompilerParams(vmem_limit_bytes=24 * 2**20),
        cost_estimate=pl.CostEstimate(
            flops=flops, bytes_accessed=bytes_accessed, transcendentals=0
        ),
    )

    def run(*arrays):
        return made(*[in_hbm(array) if i in hbm_in else array for i, array in enumerate(arrays)])

    return run


def in_hbm(array):
    return pltpu.with_memory_space_constraint(array, pltpu.HBM)


def nn(a, b):
    return lax.dot_general(a, b, (((1,), (0,)), ((), ())), preferred_element_type=F32)


def nt(a, b):
    return lax.dot_general(a, b, (((1,), (1,)), ((), ())), preferred_element_type=F32)


def tn(a, b):
    return lax.dot_general(a, b, (((0,), (0,)), ((), ())), preferred_element_type=F32)


def half_at(which, half):
    return pl.ds(pl.multiple_of(which * half, half), half)


def join_into(ref, side, own_ref, other_ref):
    half = own_ref.shape[1]
    ref[:, half_at(side, half)] = own_ref[...]
    ref[:, half_at(1 - side, half)] = other_ref[...]


def tiles(total, step):
    return [(at, min(step, total - at)) for at in range(0, total, step)]


def write_bias(bias_ref, len_ref):
    rows = bias_ref.shape[0]
    at_i = lax.broadcasted_iota(jnp.int32, (rows, rows), 0)
    at_j = lax.broadcasted_iota(jnp.int32, (rows, rows), 1)
    segment_i = jnp.zeros((rows, rows), jnp.int32)
    segment_j = jnp.zeros((rows, rows), jnp.int32)
    end = jnp.int32(0)
    for s in range(len_ref.shape[0]):
        end = end + len_ref[s]
        segment_i = segment_i + (at_i >= end).astype(jnp.int32)
        segment_j = segment_j + (at_j >= end).astype(jnp.int32)
    allowed = (segment_i == segment_j) & (at_j <= at_i)
    bias_ref[...] = jnp.where(allowed, 0.0, -1e30).astype(F32)


def one_head(pair, which):
    lane = lax.broadcasted_iota(jnp.int32, pair.shape, 1)
    keep = lane < HEAD_DIM if which == 0 else lane >= HEAD_DIM
    return jnp.where(keep, pair.astype(F32), 0.0).astype(BF16)


def forward_kernel(
    flow, len_ref, side_ref, own_ref, other_ref, gain_ref, w_ref,
    h_ref, normed_ref, qkv_ref, lse_ref, mixed_ref, inv_ref, bias_ref,
):
    side = side_ref[0]
    flow.begin(5)
    join_into(h_ref, side, own_ref, other_ref)
    values = h_ref[...].astype(F32)
    inv = lax.rsqrt(jnp.mean(values * values, axis=-1, keepdims=True) + 1e-05)
    inv_ref[...] = inv
    normed_ref[...] = (values * inv * gain_ref[...]).astype(BF16)
    flow.send(1)
    write_bias(bias_ref, len_ref)
    flow.need(5)
    for c in range(3):
        qkv_ref[c] = nn(normed_ref[...], w_ref[c]).astype(BF16)
    flow.send(2)
    for pair in range(mixed_ref.shape[1] // LANES):
        cols = slice(pair * LANES, (pair + 1) * LANES)
        total = None
        for which in range(2):
            keys = one_head(qkv_ref[1, :, cols], which)
            scores = nt(qkv_ref[0, :, cols], keys) * HEAD_DIM**-0.5 + bias_ref[...]
            row_max = jnp.max(scores, axis=-1, keepdims=True)
            lse = row_max + jnp.log(jnp.sum(jnp.exp(scores - row_max), axis=-1, keepdims=True))
            head = 2 * pair + which
            lse_ref[:, head : head + 1] = lse
            soft = jnp.exp(scores - lse).astype(BF16)
            product = nn(soft, one_head(qkv_ref[2, :, cols], which))
            total = product if total is None else total + product
        mixed_ref[:, cols] = total.astype(BF16)


def ffn_forward_kernel(
    flow, side_ref, h_ref, mixed_ref, mixed_got_ref, w_out_ref, w_out_got_ref, gain_ref, w_gu_ref, w_down_ref,
    middle_ref, normed_ref, gate_ref, up_ref, act_ref, theirs_ref, packed_ref,
):
    side = side_ref[0]
    half = packed_ref.shape[1]
    features = h_ref.shape[1]
    for at, size in tiles(features, 256):
        cols = slice(at, at + size)
        middle_ref[:, cols] = h_ref[:, cols].astype(F32) + (
            nn(mixed_ref[...], w_out_ref[:, cols]) + nn(mixed_got_ref[...], w_out_got_ref[:, cols])
        )
    flow.send(0)
    values = middle_ref[...]
    inv = lax.rsqrt(jnp.mean(values * values, axis=-1, keepdims=True) + 1e-05)
    normed_ref[...] = (values * inv * gain_ref[...]).astype(BF16)
    flow.send(1)
    for at, size in tiles(act_ref.shape[1], 256):
        cols = slice(at, at + size)
        gate = nn(normed_ref[...], w_gu_ref[0, :, cols])
        up = nn(normed_ref[...], w_gu_ref[1, :, cols])
        gate_ref[:, cols] = gate
        up_ref[:, cols] = up
        act_ref[:, cols] = (gate * jax.nn.sigmoid(gate) * up).astype(BF16)
    flow.send(2, 3, 4)
    theirs_ref[...] = nn(act_ref[...], w_down_ref[:, half_at(1 - side, half)]).astype(BF16)
    packed_ref[...] = middle_ref[:, half_at(side, half)] + nn(
        act_ref[...], w_down_ref[:, half_at(side, half)]
    )


def ffn_backward_kernel(
    flow, side_ref, co_ref, co_got_ref, gate_ref, up_ref, w_gu_ref, w_down_ref,
    upstream_ref, d_gate_ref, d_up_ref, d_part_ref,
):
    flow.begin(6, 3, 4)
    join_into(upstream_ref, side_ref[0], co_ref, co_got_ref)
    flow.send(0)
    flow.need(6, 3, 4)
    flow.begin(5)
    for at, size in tiles(gate_ref.shape[1], 256):
        cols = slice(at, at + size)
        d_act = nt(upstream_ref[...], w_down_ref[cols, :])
        gate = gate_ref[:, cols]
        sigm = jax.nn.sigmoid(gate)
        d_gate_ref[:, cols] = (
            d_act * up_ref[:, cols] * sigm * (1.0 + gate * (1.0 - sigm))
        ).astype(BF16)
        d_up_ref[:, cols] = (d_act * (gate * sigm)).astype(BF16)
    flow.need(5)
    for at, size in tiles(d_part_ref.shape[1], 256):
        cols = slice(at, at + size)
        d_part_ref[:, cols] = (
            nt(d_gate_ref[...], w_gu_ref[0, cols, :]) + nt(d_up_ref[...], w_gu_ref[1, cols, :])
        ).astype(BF16)


def backward_kernel(
    flow, len_ref, side_ref, part_ref, part_got_ref, middle_ref, up_ref, gain_f_ref, w_out_ref,
    qkv_ref, lse_ref, h_ref, inv_ref, gain_a_ref, w_ref,
    d_attn_ref, d_qkv_ref, d_mid_ref, theirs_ref, mine_ref, stat_ref, sums_ref,
    bias_ref, d_mixed_ref, d_full_ref,
):
    side = side_ref[0]
    half = d_mid_ref.shape[1]
    features = h_ref.shape[1]
    flow.begin(4, 5)
    write_bias(bias_ref, len_ref)
    flow.need(4, 5)
    flow.begin(7, 8, 9)
    middle = middle_ref[...]
    inv_f = lax.rsqrt(jnp.mean(middle * middle, axis=-1, keepdims=True) + 1e-05)
    d_normed = part_ref[...].astype(F32) + part_got_ref[...].astype(F32)
    scaled = gain_f_ref[...] * d_normed
    d_full_ref[...] = (
        up_ref[...].astype(F32)
        + inv_f * scaled
        - middle * inv_f**3 * jnp.mean(scaled * middle, axis=-1, keepdims=True)
    )
    sums_ref[1:2, :] = jnp.sum(d_normed * middle * inv_f, axis=0, keepdims=True)
    d_attn_ref[...] = d_full_ref[...].astype(BF16)
    flow.send(0)
    d_mid_ref[...] = d_full_ref[:, half_at(side, half)]
    flow.need(7, 8, 9)
    flow.begin(13, 10, 11)
    d_mixed_ref[...] = nt(d_attn_ref[...], w_out_ref[...]).astype(BF16)
    for pair in range(d_mixed_ref.shape[1] // LANES):
        cols = slice(pair * LANES, (pair + 1) * LANES)
        d_q, d_k, d_v = [], [], []
        for which in range(2):
            keys = one_head(qkv_ref[1, :, cols], which)
            head = 2 * pair + which
            scores = nt(qkv_ref[0, :, cols], keys) * HEAD_DIM**-0.5 + bias_ref[...]
            soft = jnp.exp(scores - lse_ref[:, head : head + 1])
            d_mixed = one_head(d_mixed_ref[:, cols], which)
            d_probs = nt(d_mixed, qkv_ref[2, :, cols])
            row_dots = jnp.sum(soft * d_probs, axis=-1, keepdims=True)
            d_scores = (soft * (d_probs - row_dots)).astype(BF16)
            d_q.append(nn(d_scores, keys))
            d_k.append(tn(d_scores, one_head(qkv_ref[0, :, cols], which)))
            d_v.append(tn(soft.astype(BF16), d_mixed))
        d_qkv_ref[0, :, cols] = ((d_q[0] + d_q[1]) * HEAD_DIM**-0.5).astype(BF16)
        d_qkv_ref[1, :, cols] = ((d_k[0] + d_k[1]) * HEAD_DIM**-0.5).astype(BF16)
        d_qkv_ref[2, :, cols] = (d_v[0] + d_v[1]).astype(BF16)
    flow.send(1)
    flow.need(13, 10, 11)
    for at, size in tiles(features, 256):
        cols = slice(at, at + size)
        part = nt(d_qkv_ref[0], w_ref[0, cols, :])
        part = part + nt(d_qkv_ref[1], w_ref[1, cols, :])
        d_full_ref[:, cols] = part + nt(d_qkv_ref[2], w_ref[2, cols, :])
    whole = d_full_ref[...]
    weighted = whole * h_ref[...].astype(F32)
    stat_ref[...] = jnp.sum(gain_a_ref[...] * weighted, axis=-1, keepdims=True)
    sums_ref[0:1, :] = jnp.sum(weighted * inv_ref[...], axis=0, keepdims=True)
    mine_ref[...] = d_full_ref[:, half_at(side, half)]
    theirs_ref[...] = d_full_ref[:, half_at(1 - side, half)].astype(BF16)


def by_piece(dealing_ref, seen_ref, micro, me, groups, visit):
    shift = groups.bit_length() - 1

    def clear(g, carry):
        seen_ref[g] = 0
        return carry

    def step(piece, carry):
        group = dealing_ref[micro, me * groups + piece] >> shift
        slot = seen_ref[group]
        seen_ref[group] = slot + 1
        visit(piece, group, slot)
        return carry

    lax.fori_loop(0, groups, clear, 0)
    lax.fori_loop(0, groups, step, 0)


def rows_of(piece, size):
    return pl.ds(pl.multiple_of(piece * size, size), size)


def send_kernel(place_ref, dealing_ref, array_ref, out_ref, seen_ref):
    micros, _, _ = array_ref.shape
    groups, _, size, half = out_ref.shape
    cols = half_at(place_ref[1], half)
    for m in range(micros):

        def visit(piece, group, slot):
            out_ref[group, 2 * m + slot] = array_ref[m, rows_of(piece, size), cols]

        by_piece(dealing_ref, seen_ref, m, place_ref[0], groups, visit)


def receive_kernel(slots_ref, got_ref, *out_refs):
    groups, _, size, _ = got_ref.shape
    for m, out_ref in enumerate(out_refs):

        def step(spot, carry):
            slot = slots_ref[m, spot]
            out_ref[rows_of(spot, size), :] = got_ref[slot >> 1, 2 * m + (slot & 1)]
            return carry

        lax.fori_loop(0, groups, step, 0)


def return_rows(slots_ref, rows_ref, out_ref, micro, at):
    groups, _, size, _ = out_ref.shape

    def step(spot, carry):
        slot = slots_ref[micro, spot]
        out_ref[slot >> 1, 2 * at + (slot & 1)] = rows_ref[rows_of(spot, size), :]
        return carry

    lax.fori_loop(0, groups, step, 0)


def pack_kernel(micros, slots_ref, *refs):
    packed_refs, got_refs = refs[:micros], refs[micros : 2 * micros]
    out_ref, rows_ref = refs[2 * micros :]
    for m in range(micros):
        rows_ref[...] = (packed_refs[m][...] + got_refs[m][...].astype(F32)).astype(BF16)
        return_rows(slots_ref, rows_ref, out_ref, m, m)


def finish_rows(place_ref, d_mid_ref, mine_ref, got_ref, stat_ref, stat_got_ref, inv_ref, h_ref, gain_ref):
    half = d_mid_ref.shape[1]
    inv = inv_ref[...]
    mean = (stat_ref[...] + stat_got_ref[...]) / gain_ref.shape[1]
    scaled = gain_ref[:, half_at(place_ref[1], half)] * (mine_ref[...] + got_ref[...].astype(F32))
    return d_mid_ref[...] + inv * scaled - h_ref[...].astype(F32) * (inv**3 * mean)


def finish_kernel(micro, place_ref, slots_ref, *refs):
    out_ref, rows_ref = refs[-2:]
    rows_ref[...] = finish_rows(place_ref, *refs[:-2]).astype(BF16)
    return_rows(slots_ref, rows_ref, out_ref, micro, 0)


def home_kernel(first, place_ref, dealing_ref, got_ref, *refs):
    out_refs, seen_ref = refs[:-1], refs[-1]
    groups, _, size, _ = got_ref.shape
    for i, out_ref in enumerate(out_refs):

        def visit(piece, group, slot):
            out_ref[rows_of(piece, size), :] = got_ref[group, 2 * i + slot]

        by_piece(dealing_ref, seen_ref, first + i, place_ref[0], groups, visit)


def join_kernel(place_ref, *refs):
    out_ref = refs[-1]
    half = out_ref.shape[2] // 2
    for m in range(out_ref.shape[0]):
        out_ref[m, :, half_at(place_ref[1], half)] = refs[2 * m][...]
        out_ref[m, :, half_at(1 - place_ref[1], half)] = refs[2 * m + 1][...]


def reversed_bits(value, bits):
    out = value * 0
    for b in range(bits):
        out = out + (((value >> b) & 1) << (bits - 1 - b))
    return out


def product_kernel(plan, count, bits, extra, place_ref, *refs):
    ins = refs[: count + extra]
    send_ref, keep_ref, wide_ref = refs[count + extra :]
    groups = 1 << bits
    rows = wide_ref.shape[0]
    part = rows // groups
    me, side = place_ref[0], place_ref[1]

    def spread(at, size):
        cols = pl.ds(at, size)
        for place in range(groups):
            source = reversed_bits(me * 0 + place, bits) ^ me ^ (groups - 1)
            block = wide_ref[pl.ds(pl.multiple_of(source * part, part), part), :size].astype(BF16)
            if place < groups // 2:
                send_ref[place * part : (place + 1) * part, cols] = block
            else:
                low = (place - groups // 2) * part
                keep_ref[low : low + part, cols] = block

    def one_tile(block, at_in, at_out, size):
        halves = len(block[0][0]) == 2
        for which in range(2 if halves else 1):
            total = None
            for lefts, right, plane in block:
                cols = pl.ds(at_in, size)
                factor = ins[right][:, cols] if plane is None else ins[right][plane, :, cols]
                product = tn(ins[lefts[which]][...], factor)
                total = product if total is None else total + product
            if halves:
                wide_ref[half_at(side if which == 0 else 1 - side, rows // 2), :size] = total
            else:
                wide_ref[:, :size] = total
        spread(at_out, size)

    base = 0
    for block, width in plan:
        full = width // 256

        def step(t, carry, block=block, base=base):
            at = pl.multiple_of(t * 256, 256)
            one_tile(block, at, base + at if base == 0 else pl.multiple_of(base + at, 128), 256)
            return carry

        lax.fori_loop(0, full, step, 0)
        if width % 256:
            one_tile(block, full * 256, base + full * 256, width % 256)
        base += width
    if extra:
        width = ins[-1].shape[1]
        wide_ref[:, :width] = ins[-1][...]
        spread(base, width)


def product(terms, groups, place, extra=None, stored=()):
    arrays = []

    def at(array):
        for i, known in enumerate(arrays):
            if known is array:
                return i
        arrays.append(array)
        return len(arrays) - 1

    plan = [
        ([(tuple(at(left) for left in lefts), at(right), plane) for lefts, right, plane in block],
         block[0][1].shape[-1])
        for block in terms
    ]
    count = len(arrays)
    rows = sum(left.shape[1] for left in terms[0][0][0])
    depth = sum(lefts[0].shape[0] for lefts, _, _ in terms[0])
    total = sum(width for _, width in plan)
    if extra is not None:
        arrays.append(extra)
        total += extra.shape[1]
    kernel = functools.partial(
        product_kernel, plan, count, groups.bit_length() - 1, int(extra is not None)
    )
    out = jax.ShapeDtypeStruct((rows // 2, total), BF16)
    return call(
        kernel,
        (out, out),
        [SMEM] + [VMEM] * len(arrays),
        [pltpu.VMEM((rows, 256), F32)],
        flops=2 * rows * depth * total,
        bytes_accessed=2 * rows * total + 2 * depth * (rows + total),
        hbm_in={
            1 + i: array for i, array in enumerate(arrays) if any(array is s for s in stored)
        },
    )(place, *arrays)


def halve(send, keep, groups):
    bits = groups.bit_length() - 1
    for b in range(bits):
        got = lax.ppermute(send, "dp", [(j, j ^ (1 << b)) for j in range(groups)])
        if b == bits - 1:
            return keep.astype(F32) + got.astype(F32)
        half = keep.shape[0] // 2
        send = (keep[:half].astype(F32) + got[:half].astype(F32)).astype(BF16)
        keep = (keep[half:].astype(F32) + got[half:].astype(F32)).astype(BF16)


def scatter_rows(whole, groups, me):
    rows, cols = whole.shape
    part = rows // groups
    bits = groups.bit_length() - 1
    split = whole.reshape((2,) * bits + (part, cols))
    current = split.transpose(tuple(range(bits - 1, -1, -1)) + (bits, bits + 1)).reshape(rows, cols)
    current = current.astype(BF16)
    for b in range(bits):
        half = current.shape[0] // 2
        bit = (me >> b) & 1
        send = lax.dynamic_slice_in_dim(current, (1 - bit) * half, half, 0)
        keep = lax.dynamic_slice_in_dim(current, bit * half, half, 0)
        got = lax.ppermute(send, "dp", [(j, j ^ (1 << b)) for j in range(groups)])
        total = keep.astype(F32) + got.astype(F32)
        current = total if b == bits - 1 else total.astype(BF16)
    return current


def reduced(terms, groups, place, extra=None, stored=()):
    rows = sum(left.shape[1] for left in terms[0][0][0])
    if rows // groups % 16 == 0:
        send, keep = product(terms, groups, place, extra, stored)
        return halve(send, keep, groups)

    def one(lefts, right, plane):
        left = lefts[0] if len(lefts) == 1 else joined(*lefts, place[1], 1)
        return tn(left, right if plane is None else right[plane])

    blocks = [sum(one(*term) for term in block) for block in terms]
    if extra is not None:
        blocks.append(extra)
    return scatter_rows(jnp.concatenate(blocks, axis=1), groups, place[0])


def routes(dealing, groups, me):
    _, total = dealing.shape
    blocks = dealing // groups
    spots = jnp.arange(groups)
    mine = lax.dynamic_slice_in_dim(blocks, me * groups, groups, axis=1)
    earlier = (mine[:, None, :] == mine[:, :, None]) & (spots[None, None, :] < spots[None, :, None])
    mine_slots = mine * 2 + jnp.sum(earlier.astype(jnp.int32), axis=2)
    arrivals = jnp.arange(total)
    hits = dealing[:, None, :] == (me * groups + spots)[None, :, None]
    source = jnp.sum(jnp.where(hits, arrivals[None, None, :], 0), axis=2)
    ahead = (
        (blocks[:, None, :] == me)
        & (arrivals[None, None, :] // groups == source[:, :, None] // groups)
        & (arrivals[None, None, :] < source[:, :, None])
    )
    recv_slots = source // groups * 2 + jnp.sum(ahead.astype(jnp.int32), axis=2)
    return mine_slots, recv_slots


def chosen_of(slots, groups):
    matches = slots[:, None, :] == jnp.arange(2 * groups)[None, :, None]
    return jnp.sum(jnp.where(matches, jnp.arange(groups)[None, None, :], 0), axis=2)


def rows_at(array, index):
    return array.at[index].get(mode="promise_in_bounds")


def exchange(send):
    return lax.all_to_all(send, "dp", 0, 0, tiled=True)


def slots_of(pieces, chosen):
    micros, count, rows, cols = pieces.shape
    index = (chosen + jnp.arange(micros)[:, None] * count).reshape(micros, count, 2)
    index = index.transpose(1, 0, 2).reshape(-1)
    send = rows_at(pieces.reshape(micros * count, rows, cols), index)
    return send.reshape(count, micros * 2, rows, cols)


def taken(got, slots):
    count, width, rows, cols = got.shape
    flat = got.reshape(count * width, rows, cols)
    return [
        rows_at(flat, slots[m] // 2 * width + slots[m] % 2 + 2 * m).reshape(-1, cols)
        for m in range(width // 2)
    ]


def swap(array):
    return lax.ppermute(array, "tensor", [(0, 1), (1, 0)])


def joined(own, other, side, axis):
    first = jnp.where(side == 0, own, other)
    second = jnp.where(side == 0, other, own)
    return jnp.concatenate([first, second], axis=axis)


def layer(
    inputs, cotangent, lengths, dealing, w_qkv, w_out, w_gate_up, w_down, gain_attn, gain_ffn
):
    groups = lax.axis_size("dp")
    me = lax.axis_index("dp")
    side = lax.axis_index("tensor")
    micros, rows, features = inputs.shape
    piece_rows = rows // groups
    half = features // 2
    cols = w_out.shape[0]
    hidden = w_down.shape[0]
    heads = cols // HEAD_DIM
    side_arg = side.reshape(1)
    gain_a = gain_attn.reshape(1, features)
    gain_f = gain_ffn.reshape(1, features)

    place = jnp.stack([me, side])
    mine_slots, recv_slots = routes(dealing, groups, me)
    tiled = piece_rows % 16 == 0

    def shape_of(*dims, dtype=BF16):
        return jax.ShapeDtypeStruct(dims, dtype)

    def small(kernel, out_shape, in_specs, scratch, **hbm):
        return call(kernel, out_shape, in_specs, scratch, flops=0, bytes_accessed=2**21, **hbm)

    seen = pltpu.SMEM((groups,), jnp.int32)
    half_rows = shape_of(rows, half)

    def bring(array):
        if tiled:
            send = small(
                send_kernel, shape_of(groups, 2 * micros, piece_rows, half),
                [SMEM, SMEM, VMEM], [seen], hbm_out=(0,),
            )(place, dealing, array)
            got = exchange(send)
            return small(
                receive_kernel, (half_rows,) * micros, [SMEM, VMEM], (), hbm_in={1: got},
            )(recv_slots, got)
        cut = lax.dynamic_slice_in_dim(array, side * half, half, axis=-1)
        pieces = cut.reshape(micros, groups, piece_rows, half)
        return taken(exchange(slots_of(pieces, chosen_of(mine_slots, groups))), recv_slots)

    def home(send, first):
        got = exchange(send)
        count = got.shape[1] // 2
        if tiled:
            backs = small(
                functools.partial(home_kernel, first), (half_rows,) * count,
                [SMEM, SMEM, VMEM], [seen], hbm_in={2: got},
            )(place, dealing, got)
        else:
            backs = taken(got, mine_slots[first : first + count])
        return [(back, swap(back)) for back in backs]

    def whole(pairs):
        flat = [array for pair in pairs for array in pair]
        return small(
            join_kernel, shape_of(micros, rows, features), [SMEM] + [VMEM] * len(flat), ()
        )(place, *flat)

    in_half = bring(inputs)
    co_half = bring(cotangent)
    w_out_got = swap(w_out)

    forward = call(
        forward_kernel,
        (
            shape_of(rows, features), shape_of(rows, features), shape_of(3, rows, cols),
            shape_of(rows, heads, dtype=F32), shape_of(rows, cols), shape_of(rows, 1, dtype=F32),
        ),
        [SMEM, SMEM] + [VMEM] * 4,
        [pltpu.VMEM((rows, rows), F32)],
        hbm_in={5: w_qkv},
        hbm_out=(1, 2, 3, 5),
        flow=True,
        flops=2 * rows * (features * 3 * cols + 2 * rows * cols * 2),
        bytes_accessed=2 * (3 * features * cols + rows * (3 * features + 4 * cols)),
    )
    kept = []
    for m in range(micros):
        other = swap(in_half[m])
        kept.append(forward(lengths[m, 0], side_arg, in_half[m], other, gain_a, w_qkv))

    ffn_forward = call(
        ffn_forward_kernel,
        (
            shape_of(rows, features, dtype=F32), shape_of(rows, features),
            shape_of(rows, hidden, dtype=F32), shape_of(rows, hidden, dtype=F32), shape_of(rows, hidden),
            shape_of(rows, half), shape_of(rows, half, dtype=F32),
        ),
        [SMEM] + [VMEM] * 8,
        hbm_out=(0, 1, 2, 3, 4, 6),
        flow=True,
        flops=2 * rows * features * (3 * hidden + 2 * cols),
        bytes_accessed=2 * (3 * features * hidden + 2 * features * cols + rows * (6 * features + 5 * hidden)),
    )
    fwd = []
    for m in range(micros):
        h, mixed = kept[m][0], kept[m][4]
        mixed_got = swap(mixed)
        fwd.append(
            ffn_forward(side_arg, h, mixed, mixed_got, w_out, w_out_got, gain_f, w_gate_up, w_down)
        )
    packed = [fwd[m][6] for m in range(micros)]
    packed_got = [swap(fwd[m][5]) for m in range(micros)]
    if tiled:
        send = small(
            functools.partial(pack_kernel, micros), shape_of(groups, 2 * micros, piece_rows, half),
            [SMEM] + [VMEM] * (2 * micros), [pltpu.VMEM((rows, half), BF16)], hbm_out=(0,),
        )(recv_slots, *packed, *packed_got)
    else:
        out_rows = jnp.stack([a + b.astype(F32) for a, b in zip(packed, packed_got)]).astype(BF16)
        send = slots_of(
            out_rows.reshape(micros, groups, piece_rows, half), chosen_of(recv_slots, groups)
        )
    out_full = whole(home(send, 0))

    hidden_f32 = shape_of(rows, hidden, dtype=F32)
    ffn_backward = call(
        ffn_backward_kernel,
        (
            shape_of(rows, features), shape_of(rows, hidden), shape_of(rows, hidden),
            shape_of(rows, features),
        ),
        [SMEM] + [VMEM] * 6,
        hbm_in={3: hidden_f32, 4: hidden_f32, 5: w_gate_up, 6: w_down},
        hbm_out=(0,),
        flow=True,
        flops=2 * rows * features * 3 * hidden,
        bytes_accessed=2 * (3 * features * hidden + rows * (3 * features + 6 * hidden)),
    )
    co_got = [swap(co_half[m]) for m in range(micros)]
    g_down = reduced(
        [[((co_half[m], co_got[m]), fwd[m][4], None) for m in range(micros)]], groups, place,
        stored=[fwd[m][4] for m in range(micros)],
    )
    bwd = []
    for m in range(micros):
        bwd.append(
            ffn_backward(side_arg, co_half[m], co_got[m], fwd[m][2], fwd[m][3], w_gate_up, w_down)
        )
    d_got = [swap(bwd[m][3]) for m in range(micros)]
    g_gate, g_up = [
        reduced(
            [[((fwd[m][1],), bwd[m][which], None) for m in range(micros)]], groups, place,
            stored=[fwd[m][1] for m in range(micros)],
        )
        for which in (1, 2)
    ]

    backward = call(
        backward_kernel,
        (
            shape_of(rows, features), shape_of(3, rows, cols), shape_of(rows, half, dtype=F32),
            shape_of(rows, half), shape_of(rows, half, dtype=F32), shape_of(rows, 1, dtype=F32),
            shape_of(2, features, dtype=F32),
        ),
        [SMEM, SMEM] + [VMEM] * 12,
        [
            pltpu.VMEM((rows, rows), F32),
            pltpu.VMEM((rows, cols), BF16),
            pltpu.VMEM((rows, features), F32),
        ],
        hbm_in={
            4: shape_of(rows, features, dtype=F32), 5: shape_of(rows, features), 7: w_out,
            8: shape_of(3, rows, cols), 9: shape_of(rows, heads, dtype=F32),
            10: shape_of(rows, features), 11: shape_of(rows, 1, dtype=F32), 13: w_qkv,
        },
        hbm_out=(0, 1),
        flow=True,
        flops=2 * rows * (features * 4 * cols + 2 * rows * cols * 5),
        bytes_accessed=2 * (4 * features * cols + rows * (8 * features + 9 * cols)),
    )
    tail = []
    for m in range(micros):
        h, _, qkv, lse, mixed, inv = kept[m]
        tail.append(
            backward(
                lengths[m, 0], side_arg, bwd[m][3], d_got[m], fwd[m][0], bwd[m][0], gain_f, w_out,
                qkv, lse, h, inv, gain_a, w_qkv,
            )
        )
    grad_rows = []
    for m in range(micros):
        d_mid, theirs, mine, stat = tail[m][2:6]
        finishing = (
            d_mid, mine, swap(theirs), stat, swap(stat),
            kept[m][5], in_half[m], gain_a,
        )
        if tiled:
            send = small(
                functools.partial(finish_kernel, m), shape_of(groups, 2, piece_rows, half),
                [SMEM, SMEM] + [VMEM] * 8, [pltpu.VMEM((rows, half), BF16)], hbm_out=(0,),
            )(place, recv_slots, *finishing)
        else:
            d_mid, mine, got, stat, stat_got, inv, h, gain = finishing
            gain = lax.dynamic_slice_in_dim(gain, side * half, half, axis=-1)
            d_hidden = d_mid + inv * (gain * (mine + got.astype(F32)))
            d_hidden = d_hidden - h.astype(F32) * (inv**3 * ((stat + stat_got) / features))
            pieces = d_hidden.astype(BF16).reshape(1, groups, piece_rows, half)
            send = slots_of(pieces, chosen_of(recv_slots[m : m + 1], groups))
        grad_rows += home(send, m)

    sums = sum(item[6] for item in tail)
    sums_got = swap(sums)
    share = jnp.array([[1.0], [0.5]], F32)
    extra = jnp.pad((share * (sums + sums_got)).T, ((0, 0), (0, LANES - 2)))
    products = [
        [((kept[m][1],), tail[m][1], c) for m in range(micros)] for c in range(3)
    ] + [[((tail[m][0],), kept[m][4], None) for m in range(micros)]]
    stored = [array for m in range(micros) for array in (kept[m][1], tail[m][0], tail[m][1])]
    first = reduced(products[:2], groups, place, extra, stored=stored)
    last = reduced(products[2:], groups, place, stored=stored)
    grad_qkv = jnp.stack([first[:, :cols], first[:, cols : 2 * cols], last[:, :cols]])
    gains = first[:, 2 * cols : 2 * cols + 2]
    return (
        out_full,
        whole(grad_rows),
        grad_qkv,
        last[:, cols:].T,
        jnp.stack([g_gate, g_up]),
        g_down.T,
        gains[:, 0],
        gains[:, 1],
    )


def solution(mesh):
    in_specs = (
        P(None, "dp", None),
        P(None, "dp", None),
        P(None, "dp", None),
        P(),
        P(None, None, "tensor"),
        P("tensor", None),
        P(None, None, "tensor"),
        P("tensor", None),
        P(),
        P(),
    )
    out_specs = (
        P(None, "dp", None),
        P(None, "dp", None),
        P(None, "dp", "tensor"),
        P("tensor", "dp"),
        P(None, "dp", "tensor"),
        P("tensor", "dp"),
        P("dp"),
        P("dp"),
    )
    return jax.shard_map(layer, mesh=mesh, in_specs=in_specs, out_specs=out_specs, check_vma=False)
```
